512 devices in a mesh: seq: 128 (over y, z, core), layer: 4 (over x).
Axes of the slice: x: 4, y: 4, z: 16, core: 2. Of those that a mesh axis runs over, the one named last changes fastest.
Arguments:
- tokens: bfloat16 [65536, 1024], P(('layer', 'seq')), parts along dimension 0, may hold values from -6 to 6
- routing: int32 [65536, 8], P(('layer', 'seq')), parts along dimension 0, may hold values from 0 to 127, all different within a row; in each aligned block of 128 rows (0 to 127, 128 to 255, ...) at most 16 rows name the same one
- gate_weight: bfloat16 [512, 1024, 384], P(('layer', 'seq')), parts along dimension 0, may hold values from -0.1875 to 0.1875
- up_weight: bfloat16 [512, 1024, 384], P(('layer', 'seq')), parts along dimension 0, may hold values from -0.1875 to 0.1875
- down_weight: bfloat16 [512, 384, 1024], P(('layer', 'seq')), parts along dimension 0, may hold values from -6 to 6
- cluster_of: int32 [512], P('layer'), parts along dimension 0, may hold values from 0 to 63, as said below
- owners: int32 [256], P('layer'), parts along dimension 0, may hold values from 0 to 127, as said below
Outputs:
- differences: bfloat16 [512, 384, 1024], P(('layer', 'seq')), parts along dimension 0
- merged_slots: bfloat16 [512, 384, 1024], P(('layer', 'seq')), parts along dimension 0
The draws below stay inside these ranges and needn't reach their ends.
There are 4 independent parts, one for each index of `layer`. The reference program is written for one: setup_inputs(seed, part) draws one part's arguments, and reference() takes and returns one part's arrays. A program takes and returns all parts, laid end to end along the dimension named above; each array names one. Nothing has to cross between parts.
Inputs may be any that keep to these rules, and one draw needn't show every extreme that they name: `routing`: each row names 8 different experts. Among the 128 rows of one device no expert is named more than 16 times, a bound that some block reaches. `cluster_of`: every cluster has at least one member. Different clusters have different owners.
All inputs are finite; a program needn't handle non-finite values.
Results may differ from the reference program's by a relative error of at most 0.0058.
Values may be sent and summed in bfloat16 or wider, within the bound.
A program may use at most 64 MiB of HBM per device.

```python
import math
import jax
import jax.numpy as jnp
import numpy as np
from jax import lax

D = 1024
F = 384
TOPK = 8
OWN = 1
TOK_DEV = 128
EXPERTS = 128
CLUSTERS = 64
CAP = 16
TOKENS = 16384
N_SEQ = 128


def draw_cluster_of(key, part):
    shuffled = jax.random.permutation(jax.random.fold_in(key, 11), EXPERTS)
    further = jax.random.randint(jax.random.fold_in(key, 12), (EXPERTS,), 0, CLUSTERS)
    return jnp.where(shuffled < CLUSTERS, shuffled, further).astype(jnp.int32)


def draw_owners(key, part):
    shuffled = jax.random.permutation(jax.random.fold_in(key, 21), EXPERTS)
    return shuffled[:CLUSTERS].astype(jnp.int32)


def levels(stream_key, extent, cuts, low, largest):
    def one(dim, parts):
        draws = jax.random.uniform(jax.random.fold_in(jax.random.fold_in(stream_key, 6), dim), (parts,), jnp.float32, low / len(cuts), largest / len(cuts))
        return jnp.repeat(jnp.exp(draws), extent[dim] // parts).reshape((-1,) + (1,) * (len(extent) - dim - 1))

    gain = one(*cuts[0])
    for cut in cuts[1:]:
        gain = gain * one(*cut)
    return gain


def assign_block(key, own, number, rows, count, top, reach, slope):
    order = jax.random.permutation(key, count)
    crowded, usual = portions_of(count, rows * top, reach, slope, True), portions_of(count, rows * top, reach, slope, False)
    places = jnp.arange(count)

    def named(tallies, turn):
        used = int((tallies > 0).sum())
        fixed = max(1, used // 4)
        passed = fixed + (places - fixed + turn * (used - fixed)) % max(1, count - fixed)
        return jnp.zeros((count,), jnp.int32).at[order[jnp.where(places < fixed, places, passed)]].set(jnp.asarray(tallies, jnp.int32))

    tallies = jnp.where(number % 4 == 0, named(crowded, number // 4), named(usual, number - number // 4 - 1))
    mixed = jax.random.permutation(jax.random.fold_in(own, 3), count)
    source_of, sink = mixed[0:count // 2 * 2:2], mixed[1:count // 2 * 2:2]
    slack = jnp.minimum(tallies[source_of] - 1, reach - tallies[sink]) // 2
    slack = jnp.where((source_of == order[0]) | (sink == order[0]) | (tallies[sink] == 0), 0, jnp.maximum(slack, 0))
    passed = jax.random.randint(jax.random.fold_in(own, 4), (count // 2,), 0, 1 << 20) % (slack + 1)
    tallies = tallies.at[source_of].add(-passed).at[sink].add(passed)
    members = jnp.searchsorted(jnp.cumsum(tallies), jnp.arange(rows * top), side="right").astype(jnp.int32)
    grid = members.reshape(top, rows).T
    grid = grid[jax.random.permutation(jax.random.fold_in(own, 1), rows)]
    turn = jax.random.randint(jax.random.fold_in(own, 2), (rows, 1), 0, top)
    return jnp.take_along_axis(grid, (jnp.arange(top)[None, :] + turn) % top, axis=1)


def portions_of(count, total, most, lean, full):
    weights = [(1 << 20) // math.isqrt(rank ** lean) + 1 for rank in range(1, count + 1)]
    largest = most if full else min(most, max(-(-total // count), total * weights[0] // sum(weights)))
    least = 1 if total - largest >= count - 1 else 0
    counts, surplus = [largest] + [least] * (count - 1), total - largest - least * (count - 1)
    while surplus > 0:
        candidates = [i for i in range(1, count) if counts[i] < largest] or [i for i in range(1, count) if counts[i] < most]
        pool, remaining = sum([weights[i] for i in candidates]), surplus
        for i in candidates:
            extra = min(most - counts[i], max(1, remaining * weights[i] // pool), surplus)
            counts[i] = counts[i] + extra
            surplus = surplus - extra
    return np.array(counts)


def scatter_about(key, shape, width, reach, cuts=(), kind=jnp.bfloat16):
    factor_of = levels(key, shape, cuts, -0.22, 0.18) if cuts else 1.0
    array = jax.random.normal(key, shape, jnp.float32) * width * factor_of
    return jnp.minimum(jnp.maximum(array, -reach), reach).astype(kind)


def setup_inputs(seed: int = 0, part: int = 0) -> dict:
    arg_keys = jax.random.split(jax.random.key(seed), 8)
    own_keys = jax.random.split(jax.random.fold_in(arg_keys[7], part), 8)
    tokens = scatter_about(own_keys[0], (TOKENS, D), 1.0, 6.0, ((0, 128),))
    routing_keys = jax.random.split(jax.random.fold_in(own_keys[1], 1), TOKENS // TOK_DEV)
    routing_turns = jax.random.permutation(jax.random.fold_in(own_keys[1], 3), TOKENS // TOK_DEV)
    routing = jax.vmap(lambda own, number: assign_block(jax.random.fold_in(own_keys[1], 2), own, number, TOK_DEV, EXPERTS, TOPK, CAP, 2))(routing_keys, routing_turns).reshape((TOKENS, TOPK))
    gate_weight = scatter_about(own_keys[2], (EXPERTS, D, F), D ** -0.5, 0.1875, ((0, 128),))
    up_weight = scatter_about(own_keys[3], (EXPERTS, D, F), D ** -0.5, 0.1875, ((0, 128),))
    down_weight = scatter_about(own_keys[4], (EXPERTS, F, D), 1.0, 6.0, ((0, 128),))
    cluster_of = draw_cluster_of(jax.random.fold_in(jax.random.fold_in(arg_keys[7], part), 71), part)
    owners = draw_owners(jax.random.fold_in(jax.random.fold_in(arg_keys[7], part), 71), part)
    return {"tokens": tokens, "routing": routing, "gate_weight": gate_weight, "up_weight": up_weight, "down_weight": down_weight, "cluster_of": cluster_of, "owners": owners}


ridge_weight = 32.0

def cluster_slots(owners):
    count = owners.shape[0]
    same_owner = owners[:, None] == owners[None, :]
    earlier = lax.broadcasted_iota(jnp.int32, (count, count), 1) < lax.broadcasted_iota(jnp.int32, (count, count), 0)
    ranking = jnp.sum((same_owner & earlier).astype(jnp.int32), axis=1)
    return owners * OWN + ranking

def solve_merged(pair):
    grams, products = pair
    factor = jnp.linalg.cholesky(grams)
    return jax.scipy.linalg.cho_solve((factor, True), products)

def reference(tokens, routing, gate_weight, up_weight, down_weight, cluster_of, owners):
    entries = TOK_DEV * TOPK
    flat_ids = routing.reshape(N_SEQ, entries)
    onehot = (flat_ids[:, :, None] == jnp.arange(EXPERTS, dtype=jnp.int32)[None, None, :]).astype(jnp.int32)
    before = jnp.cumsum(onehot, axis=1) - onehot
    ranking = jnp.sum(before * onehot, axis=2)
    block_ids = jnp.arange(N_SEQ, dtype=jnp.int32)[:, None]
    position = flat_ids * (N_SEQ * CAP) + block_ids * CAP + ranking
    source = block_ids * TOK_DEV + jnp.arange(entries, dtype=jnp.int32)[None, :] // TOPK
    table = jnp.full((EXPERTS * N_SEQ * CAP,), -1, jnp.int32)
    table = table.at[position.reshape(-1)].set(source.reshape(-1).astype(jnp.int32))
    table = table.reshape(EXPERTS, N_SEQ * CAP)
    identity_f = jnp.eye(F, dtype=jnp.float32)

    def per_expert(items):
        row_index, gate_block, up_block, down_block = items
        present = row_index >= 0
        picked = tokens[jnp.maximum(row_index, 0).astype(jnp.int32)]
        rows = jnp.where(present[:, None], picked, jnp.zeros((), jnp.bfloat16))
        gate = jnp.dot(rows.astype(jnp.float32), gate_block.astype(jnp.float32), preferred_element_type=jnp.float32)
        upward = jnp.dot(rows.astype(jnp.float32), up_block.astype(jnp.float32), preferred_element_type=jnp.float32)
        hidden = (jax.nn.silu(gate) * upward).astype(jnp.bfloat16)
        gram_matrix = jnp.dot(hidden.T.astype(jnp.float32), hidden.astype(jnp.float32), preferred_element_type=jnp.float32) + ridge_weight * identity_f
        product_rows = jnp.dot(gram_matrix, down_block.astype(jnp.float32), precision=lax.Precision.HIGHEST)
        return (gram_matrix, product_rows)
    grams, products = lax.map(per_expert, (table, gate_weight, up_weight, down_weight))
    gram_sums = jax.ops.segment_sum(grams, cluster_of, num_segments=CLUSTERS)
    product_sums = jax.ops.segment_sum(products, cluster_of, num_segments=CLUSTERS)
    merged = lax.map(solve_merged, (gram_sums, product_sums)).astype(jnp.bfloat16)
    differences = (merged[cluster_of].astype(jnp.float32) - down_weight.astype(jnp.float32)).astype(jnp.bfloat16)
    slots = cluster_slots(owners)
    merged_slots = jnp.zeros((N_SEQ * OWN, F, D), jnp.bfloat16).at[slots].set(merged)
    return (differences, merged_slots)
```

```python
import jax
import jax.numpy as jnp
from jax import lax
from jax.experimental import pallas as pl
from jax.experimental.pallas import tpu as pltpu
from jax.sharding import Mesh
from jax.sharding import PartitionSpec as P

OWN = 1
SEQ = ("seq_0", "seq_1", "seq_2")
PLANE = ("seq_0", "seq_2")
LAYER_SEQ = ("layer", "seq_0", "seq_1", "seq_2")
HI = lax.Precision.HIGHEST
F32 = jnp.float32
BF16 = jnp.bfloat16

ridge_weight = 32.0
LANES = 128
BLOCKS = ((0, 0), (1, 0), (1, 1), (2, 0), (2, 1), (2, 2))


def dot(a, b, dims=((1,), (0,)), precision=None):
    return lax.dot_general(a, b, (dims, ((), ())), preferred_element_type=F32, precision=precision)


def select_kernel(experts_ref, routing_ref, tokens_ref, out_ref):
    rows = tokens_ref.shape[1]
    count = experts_ref.shape[0]
    capacity = out_ref.shape[2]
    ids = routing_ref[0]
    experts = experts_ref[...]
    named = jnp.zeros((count, rows), F32)
    for k in range(ids.shape[0]):
        named += (ids[k : k + 1, :] == experts).astype(F32)
    upper = (
        lax.broadcasted_iota(jnp.int32, (rows, rows), 0)
        < lax.broadcasted_iota(jnp.int32, (rows, rows), 1)
    ).astype(BF16)
    before = dot(named.astype(BF16), upper)
    slot = jnp.where(named > 0.0, before, -1.0)
    place = lax.broadcasted_iota(jnp.int32, (capacity, rows), 0).astype(F32)
    tokens = tokens_ref[0]
    for j in range(count):
        picker = (slot[j : j + 1, :] == place).astype(BF16)
        out_ref[j, 0] = dot(picker, tokens).astype(BF16)


def select_rows(experts, routing_all, tokens_all, capacity):
    blocks, rows, width = tokens_all.shape
    count = experts.shape[0]
    return pl.pallas_call(
        select_kernel,
        out_shape=jax.ShapeDtypeStruct((count, blocks, capacity, width), BF16),
        grid=(blocks,),
        in_specs=[
            pl.BlockSpec((count, rows), lambda b: (0, 0)),
            pl.BlockSpec((1, routing_all.shape[1], rows), lambda b: (b, 0, 0)),
            pl.BlockSpec((1, rows, width), lambda b: (b, 0, 0)),
        ],
        out_specs=pl.BlockSpec((count, 1, capacity, width), lambda b: (0, b, 0, 0)),
    )(jnp.broadcast_to(experts[:, None], (count, rows)), routing_all, tokens_all)


def gram_kernel(rows_ref, gate_ref, up_ref, out_ref):
    step = pl.program_id(0)

    @pl.when(step == 0)
    def _():
        out_ref[...] = jnp.zeros_like(out_ref)

    rows = rows_ref[...]
    gate = dot(rows, gate_ref[...])
    upward = dot(rows, up_ref[...])
    hidden = (gate / (1.0 + jnp.exp(-gate)) * upward).astype(BF16)
    for b, (i, j) in enumerate(BLOCKS):
        left = hidden[:, i * LANES : (i + 1) * LANES]
        right = hidden[:, j * LANES : (j + 1) * LANES]
        out_ref[:, b * LANES : (b + 1) * LANES] += dot(left, right, ((0,), (0,)))

    @pl.when(step == pl.num_programs(0) - 1)
    def _():
        eye = (
            lax.broadcasted_iota(jnp.int32, (LANES, LANES), 0)
            == lax.broadcasted_iota(jnp.int32, (LANES, LANES), 1)
        ).astype(F32)
        for b, (i, j) in enumerate(BLOCKS):
            if i == j:
                out_ref[:, b * LANES : (b + 1) * LANES] += ridge_weight * eye


def packed_gram(rows, gate, up, tile=512):
    count, width = rows.shape
    hidden_units = gate.shape[1]
    return pl.pallas_call(
        gram_kernel,
        out_shape=jax.ShapeDtypeStruct((LANES, len(BLOCKS) * LANES), F32),
        grid=(count // tile,),
        in_specs=[
            pl.BlockSpec((tile, width), lambda s: (s, 0)),
            pl.BlockSpec((width, hidden_units), lambda s: (0, 0)),
            pl.BlockSpec((width, hidden_units), lambda s: (0, 0)),
        ],
        out_specs=pl.BlockSpec((LANES, len(BLOCKS) * LANES), lambda s: (0, 0)),
    )(rows, gate, up)


def inverse(block):
    size = block.shape[0]
    groups = size // 8
    lanes = lax.broadcasted_iota(jnp.int32, (8, size), 1)
    subs = lax.broadcasted_iota(jnp.int32, (8, size), 0)
    parts = [block[8 * g : 8 * g + 8, :] for g in range(groups)]
    for k in range(size):
        own, row = k // 8, k % 8
        pivot_row = jnp.broadcast_to(parts[own][row : row + 1, :], (8, size))
        pivot = jnp.broadcast_to(pivot_row[:, k : k + 1], (8, size))
        scaled = jnp.where(lanes == k, 1.0, pivot_row) / pivot
        fresh = []
        for g in range(groups):
            column = jnp.broadcast_to(parts[g][:, k : k + 1], (8, size))
            part = jnp.where(lanes == k, 0.0, parts[g]) - column * scaled
            if g == own:
                part = jnp.where(subs == row, scaled, part)
            fresh.append(part)
        parts = fresh
    return jnp.concatenate(parts, axis=0)


def solve_kernel(sum_ref, own_ref, down_ref, out_ref, work_ref, right_ref):
    def block(ref, b):
        return ref[:, b * LANES : (b + 1) * LANES]

    a00, a10, a11, a20, a21, a22 = (block(sum_ref, b) for b in range(6))
    nt = ((1,), (1,))
    tn = ((0,), (0,))

    work_ref[0] = a00
    g = [block(own_ref, b) for b in range(6)]
    right_ref[0] = jnp.concatenate([g[0], g[1].T, g[3].T], axis=1)
    right_ref[1] = jnp.concatenate([g[1], g[2], g[4].T], axis=1)
    right_ref[2] = jnp.concatenate([g[3], g[4], g[5]], axis=1)

    d0 = inverse(work_ref[0])
    l10 = dot(a10, d0, precision=HI)
    l20 = dot(a20, d0, precision=HI)
    a11 = a11 - dot(l10, a10, nt, precision=HI)
    a21 = a21 - dot(l20, a10, nt, precision=HI)
    a22 = a22 - dot(l20, a20, nt, precision=HI)
    d1 = inverse(a11)
    l21 = dot(a21, d1, precision=HI)
    a22 = a22 - dot(l21, a21, nt, precision=HI)
    d2 = inverse(a22)

    y0 = right_ref[0]
    y1 = right_ref[1] - dot(l10, y0, precision=HI)
    y2 = right_ref[2] - dot(l20, y0, precision=HI) - dot(l21, y1, precision=HI)
    x2 = dot(d2, y2, precision=HI)
    x1 = dot(d1, y1, precision=HI) - dot(l21, x2, tn, precision=HI)
    x0 = (
        dot(d0, y0, precision=HI)
        - dot(l10, x1, tn, precision=HI)
        - dot(l20, x2, tn, precision=HI)
    )
    for i, x in enumerate((x0, x1, x2)):
        high = x.astype(BF16)
        low = (x - high.astype(F32)).astype(BF16)
        down = down_ref[...]
        out_ref[i * LANES : (i + 1) * LANES, :] = (dot(high, down) + dot(low, down)).astype(BF16)


def member_part(gram_sum, gram_own, down):
    rows, width = down.shape
    return pl.pallas_call(
        solve_kernel,
        out_shape=jax.ShapeDtypeStruct((rows, width), BF16),
        scratch_shapes=[
            pltpu.VMEM((1, LANES, LANES), F32),
            pltpu.VMEM((3, LANES, 3 * LANES), F32),
        ],
    )(gram_sum, gram_own, down)


def cluster_slots(owners):
    count = owners.shape[0]
    same_owner = owners[:, None] == owners[None, :]
    earlier = lax.broadcasted_iota(jnp.int32, (count, count), 1) < lax.broadcasted_iota(
        jnp.int32, (count, count), 0
    )
    ranking = jnp.sum((same_owner & earlier).astype(jnp.int32), axis=1)
    return owners * OWN + ranking


def exchange(array, axes):
    return lax.all_to_all(array, axes, split_axis=0, concat_axis=0, tiled=True)


def body(tokens, routing, gate_weight, up_weight, down_weight, cluster_of, owners):
    ys, zs, cores = (lax.axis_size(a) for a in SEQ)
    seq_count = ys * zs * cores
    rows_dev, width = tokens.shape
    topk = routing.shape[1]
    experts = cluster_of.shape[0]
    clusters = owners.shape[0]
    hidden_units = gate_weight.shape[2]
    capacity = min(rows_dev, max(2, 2 * rows_dev * topk // experts))
    out_width = down_weight.shape[2]

    slots = cluster_slots(owners)
    member_match = cluster_of[:, None] == lax.broadcasted_iota(jnp.int32, (experts, clusters), 1)
    member_slot = jnp.sum(jnp.where(member_match, slots[None, :], 0), axis=1)
    same_cluster = (cluster_of[:, None] == cluster_of[None, :]).astype(F32)
    slot_range = lax.broadcasted_iota(jnp.int32, (seq_count * OWN, experts), 0)
    route_owner = (slot_range == member_slot[None, :]).astype(F32)

    routing_all = lax.all_gather(routing.T, "seq_1")
    tokens_all = lax.all_gather(tokens, "seq_1")
    plane = jnp.arange(ys * cores, dtype=jnp.int32)
    plane_experts = (
        (plane // cores) * (zs * cores) + lax.axis_index("seq_1") * cores + plane % cores
    )
    chosen = select_rows(plane_experts, routing_all, tokens_all, capacity)
    arrived = exchange(chosen, PLANE).reshape(-1, width)

    own_gram = packed_gram(arrived, gate_weight[0], up_weight[0])
    pieces = exchange(own_gram, SEQ)
    summed = jnp.dot(same_cluster, pieces, precision=HI)
    gram_sum = exchange(summed, SEQ)
    part = member_part(gram_sum, own_gram, down_weight[0])

    wide = out_width // LANES
    high = hidden_units * wide // seq_count
    tall = hidden_units // high
    chunks = part.reshape(tall, high, wide, LANES).transpose(0, 2, 1, 3)
    chunks = exchange(chunks.reshape(seq_count, high, LANES), SEQ)
    router = jnp.stack([same_cluster, route_owner], axis=1).astype(BF16)
    merged = jnp.einsum("qwe,erk->qwrk", router, chunks, preferred_element_type=F32).astype(BF16)
    merged = exchange(merged, SEQ)
    merged = merged.reshape(tall, wide, 2, high, LANES).transpose(2, 0, 3, 1, 4)
    merged = merged.reshape(2, 1, hidden_units, out_width)
    differences = (merged[0].astype(F32) - down_weight.astype(F32)).astype(BF16)
    return (differences, merged[1])


def solution(mesh):
    finer = Mesh(
        mesh.devices.reshape(4, 16, 2, mesh.shape["layer"]), ("seq_0", "seq_1", "seq_2", "layer")
    )
    return jax.shard_map(
        body,
        mesh=finer,
        in_specs=(
            P(LAYER_SEQ, None),
            P(LAYER_SEQ, None),
            P(LAYER_SEQ, None, None),
            P(LAYER_SEQ, None, None),
            P(LAYER_SEQ, None, None),
            P("layer"),
            P("layer"),
        ),
        out_specs=(P(LAYER_SEQ, None, None), P(LAYER_SEQ, None, None)),
        check_vma=False,
    )
```

```python
import functools

import jax
import jax.numpy as jnp
from jax import lax
from jax.experimental import pallas as pl
from jax.experimental.pallas import tpu as pltpu
from jax.sharding import Mesh
from jax.sharding import PartitionSpec as P

OWN = 1
SEQ = ("seq_0", "seq_1", "seq_2")
PLANE = ("seq_0", "seq_2")
LAYER_SEQ = ("layer", "seq_0", "seq_1", "seq_2")
HI = lax.Precision.HIGHEST
F32 = jnp.float32
BF16 = jnp.bfloat16
MESH = pl.DeviceIdType.MESH

ridge_weight = 32.0
LANES = 128
BLOCKS = ((0, 0), (1, 0), (1, 1), (2, 0), (2, 1), (2, 2))


def dot(a, b, dims=((1,), (0,)), precision=None):
    return lax.dot_general(a, b, (dims, ((), ())), preferred_element_type=F32, precision=precision)


def tokens_kernel(sizes, tokens_ref, routing_ref, out_ref, held, ids, stage,
                  tok_send, tok_recv, ids_send, ids_recv, plane_send, plane_recv):
    ys, zs, cores = sizes
    rows = tokens_ref.shape[0]
    count, blocks, capacity, width = out_ref.shape
    halves = 2
    half = rows // halves
    y, z, c = (lax.axis_index(a) for a in SEQ)
    right, left = lax.rem(z + 1, zs), lax.rem(z + zs - 1, zs)
    peers = []
    for p in range(1, count):
        peers.append({"seq_0": lax.rem(y + p // cores, ys), "seq_2": lax.rem(c + p % cores, cores)})

    barrier = pltpu.get_barrier_semaphore()
    for target in [{"seq_1": right}, {"seq_1": left}] + peers:
        pl.semaphore_signal(barrier, inc=1, device_id=target, device_id_type=MESH)

    place = lax.broadcasted_iota(jnp.int32, (count, rows), 0)
    experts = (
        lax.rem(y + place // cores, ys) * (zs * cores) + z * cores + lax.rem(c + lax.rem(place, cores), cores)
    )
    upper = (
        lax.broadcasted_iota(jnp.int32, (rows, rows), 0)
        < lax.broadcasted_iota(jnp.int32, (rows, rows), 1)
    ).astype(BF16)
    slot_of = lax.broadcasted_iota(jnp.int32, (capacity, rows), 0).astype(F32)

    def token_copy(source, slot, part, target):
        rng = pl.ds(part * half, half)
        return pltpu.make_async_remote_copy(
            src_ref=source.at[rng, :], dst_ref=held.at[slot, rng, :],
            send_sem=tok_send.at[slot, part], recv_sem=tok_recv.at[slot, part],
            device_id={"seq_1": target}, device_id_type=MESH)

    def ids_copy(source, slot, target):
        return pltpu.make_async_remote_copy(
            src_ref=source, dst_ref=ids.at[slot],
            send_sem=ids_send.at[slot], recv_sem=ids_recv.at[slot],
            device_id={"seq_1": target}, device_id_type=MESH)

    def plane_copy(slot, p):
        return pltpu.make_async_remote_copy(
            src_ref=stage.at[slot, p - 1], dst_ref=out_ref.at[p, slot],
            send_sem=plane_send.at[p], recv_sem=plane_recv.at[p],
            device_id=peers[p - 1], device_id_type=MESH)

    def choose(slot, tokens, names):
        named = jnp.zeros((count, rows), F32)
        for k in range(names.shape[0]):
            named += (names[k : k + 1, :] == experts).astype(F32)
        before = dot(named.astype(BF16), upper)
        where = jnp.where(named > 0.0, before, -1.0)
        picker = jnp.concatenate(
            [(where[p : p + 1, :] == slot_of).astype(BF16) for p in range(count)], axis=0)
        chosen = dot(picker, tokens).astype(BF16)
        out_ref[0, slot] = chosen[:capacity]
        for p in range(1, count):
            stage[slot, p - 1] = chosen[p * capacity : (p + 1) * capacity]
        for p in range(1, count):
            plane_copy(slot, p).start()

    pl.semaphore_wait(barrier, count + 1)
    ups = zs // 2
    for part in range(halves):
        token_copy(tokens_ref, 1, part, right).start()
        token_copy(tokens_ref, zs - 1, part, left).start()
    ids_copy(routing_ref, 1, right).start()
    ids_copy(routing_ref, zs - 1, left).start()
    choose(0, tokens_ref[...], routing_ref[...])

    def take(slot, onward, target, last):
        ids_copy(ids.at[slot], slot, target).wait_recv()
        if not last:
            ids_copy(ids.at[slot], onward, target).start()
        for part in range(halves):
            token_copy(held.at[slot], slot, part, target).wait_recv()
            if not last:
                token_copy(held.at[slot], onward, part, target).start()

    def step(d, _):
        take(d, d + 1, right, False)
        take(zs - d, zs - d - 1, left, False)
        choose(d, held[d], ids[d])
        choose(zs - d, held[zs - d], ids[zs - d])
        return 0

    lax.fori_loop(1, ups - 1, step, 0)
    take(ups - 1, ups, right, False)
    take(ups + 1, ups, left, True)
    choose(ups - 1, held[ups - 1], ids[ups - 1])
    choose(ups + 1, held[ups + 1], ids[ups + 1])
    take(ups, 0, right, True)
    choose(ups, held[ups], ids[ups])

    def sent(slot, _):
        for part in range(halves):
            token_copy(tokens_ref, slot, part, right).wait_send()
        ids_copy(routing_ref, slot, right).wait_send()
        return 0

    lax.fori_loop(1, zs, sent, 0)
    for p in range(1, count):
        whole = pltpu.make_async_remote_copy(
            src_ref=out_ref.at[p], dst_ref=out_ref.at[p],
            send_sem=plane_send.at[p], recv_sem=plane_recv.at[p],
            device_id=peers[p - 1], device_id_type=MESH)
        whole.wait()


def spread_tokens(tokens, routing_t, sizes, capacity, cid):
    ys, zs, cores = sizes
    rows, width = tokens.shape
    count = ys * cores
    vm = pl.BlockSpec(memory_space=pltpu.VMEM)
    return pl.pallas_call(
        functools.partial(tokens_kernel, sizes),
        out_shape=jax.ShapeDtypeStruct((count, zs, capacity, width), BF16),
        in_specs=[vm, vm], out_specs=vm,
        scratch_shapes=[
            pltpu.VMEM((zs, rows, width), BF16),
            pltpu.VMEM((zs,) + routing_t.shape, jnp.int32),
            pltpu.VMEM((zs, count - 1, capacity, width), BF16),
            pltpu.SemaphoreType.DMA((zs, 2)), pltpu.SemaphoreType.DMA((zs, 2)),
            pltpu.SemaphoreType.DMA((zs,)), pltpu.SemaphoreType.DMA((zs,)),
            pltpu.SemaphoreType.DMA((count,)), pltpu.SemaphoreType.DMA((count,)),
        ],
        compiler_params=pltpu.CompilerParams(collective_id=cid, has_side_effects=True),
    )(tokens, routing_t)


def partner(i, sizes, here, sign):
    ys, zs, cores = sizes
    y, z, c = here
    dc = lax.rem(i, cores)
    rest = i // cores
    dy = lax.rem(rest, ys)
    zi = rest // ys
    dz = lax.rem(lax.rem(zi, 2) * ((zi + 1) // 2) + (1 - lax.rem(zi, 2)) * (zs - zi // 2), zs)
    if sign > 0:
        to = (lax.rem(y + dy, ys), lax.rem(z + dz, zs), lax.rem(c + dc, cores))
    else:
        to = (lax.rem(y + ys - dy, ys), lax.rem(z + zs - dz, zs), lax.rem(c + cores - dc, cores))
    return to, dict(zip(SEQ, to)), (to[0] * zs + to[1]) * cores + to[2]


def greet(n, sizes, here):
    barrier = pltpu.get_barrier_semaphore()

    def hello(i, _):
        _, to, _ = partner(i, sizes, here, 1)
        pl.semaphore_signal(barrier, inc=1, device_id=to, device_id_type=MESH)
        return 0

    lax.fori_loop(1, n, hello, 0)
    pl.semaphore_wait(barrier, n - 1)


def swap(n, sizes, here, src, dst, send_sem, recv_sem, local_sem):
    me = (here[0] * sizes[1] + here[1]) * sizes[2] + here[2]
    own = pltpu.make_async_copy(src(me), dst(me), local_sem)
    own.start()

    def send(i, _):
        _, to, index = partner(i, sizes, here, 1)
        pltpu.make_async_remote_copy(
            src_ref=src(index), dst_ref=dst(me), send_sem=send_sem, recv_sem=recv_sem,
            device_id=to, device_id_type=MESH).start()
        return 0

    lax.fori_loop(1, n, send, 0)
    own.wait()


def grams_kernel(sizes, blocks, gram_ref, same_ref, out_ref, a, b, c, d, send_sem, recv_sem, local_sem):
    n = sizes[0] * sizes[1] * sizes[2]
    lanes = 128
    here = tuple(lax.axis_index(x) for x in SEQ)
    for k in range(blocks):
        a[pl.ds(k, lanes, stride=8), :] = gram_ref[:, k * lanes : (k + 1) * lanes]
    greet(n, sizes, here)

    def tile(ref):
        return lambda i: ref.at[pl.ds(pl.multiple_of(i * 8, 8), blocks), :]

    def settle(k, ref):
        whole = pltpu.make_async_remote_copy(
            src_ref=ref.at[pl.ds(0, (n - 1) * blocks), :], dst_ref=ref.at[pl.ds(0, (n - 1) * blocks), :],
            send_sem=send_sem.at[k], recv_sem=recv_sem.at[k], device_id={"seq_0": 0}, device_id_type=MESH)
        whole.wait()

    swap(n, sizes, here, tile(a), tile(b), send_sem.at[0], recv_sem.at[0], local_sem)
    settle(0, b)
    same = same_ref[...]
    for k in range(blocks):
        c[pl.ds(k, lanes, stride=8), :] = dot(same, b[pl.ds(k, lanes, stride=8), :], precision=HI)
    swap(n, sizes, here, tile(c), tile(d), send_sem.at[1], recv_sem.at[1], local_sem)
    settle(1, d)
    for k in range(blocks):
        out_ref[:, k * lanes : (k + 1) * lanes] = d[pl.ds(k, lanes, stride=8), :]


def exchange_grams(gram, same, sizes, cid):
    blocks = gram.shape[1] // 128
    n = sizes[0] * sizes[1] * sizes[2]
    vm = pl.BlockSpec(memory_space=pltpu.VMEM)
    big = pltpu.VMEM((n * 8, 128), F32)
    return pl.pallas_call(
        functools.partial(grams_kernel, sizes, blocks),
        out_shape=jax.ShapeDtypeStruct(gram.shape, F32),
        in_specs=[vm, vm], out_specs=vm,
        scratch_shapes=[big, big, big, big, pltpu.SemaphoreType.DMA((2,)), pltpu.SemaphoreType.DMA((2,)), pltpu.SemaphoreType.DMA],
        compiler_params=pltpu.CompilerParams(collective_id=cid, has_side_effects=True),
    )(gram, same)


def parts_kernel(sizes, parts_ref, router_ref, out_ref, got, wide, mixed, back, send_sem, recv_sem, local_sem):
    n = sizes[0] * sizes[1] * sizes[2]
    lanes = 128
    high = parts_ref.shape[1]
    ways = router_ref.shape[0] // n
    here = tuple(lax.axis_index(x) for x in SEQ)
    greet(n, sizes, here)

    def settle(k, ref):
        whole = pltpu.make_async_remote_copy(
            src_ref=ref.at[pl.ds(0, n - 1)], dst_ref=ref.at[pl.ds(0, n - 1)],
            send_sem=send_sem.at[k], recv_sem=recv_sem.at[k], device_id={"seq_0": 0}, device_id_type=MESH)
        whole.wait()

    swap(n, sizes, here, lambda i: parts_ref.at[i], lambda i: got.at[i], send_sem.at[0], recv_sem.at[0], local_sem)
    settle(0, got)

    def widen(i, _):
        wide[pl.ds(pl.multiple_of(i * high, 8), high), :] = got[i].astype(F32)
        return 0

    lax.fori_loop(0, n, widen, 0, unroll=8)
    router = router_ref[...]

    def mix(r, _):
        x = wide[pl.ds(r, n, stride=high), :].astype(BF16)
        mixed[pl.ds(r, ways * n, stride=high), :] = dot(router, x)
        return 0

    lax.fori_loop(0, high, mix, 0, unroll=4)

    def narrow(i, _):
        for w in range(ways):
            back[i, w] = mixed[pl.ds(pl.multiple_of((i * ways + w) * high, 8), high), :].astype(BF16)
        return 0

    lax.fori_loop(0, n, narrow, 0, unroll=4)
    swap(n, sizes, here, lambda i: back.at[i], lambda i: out_ref.at[i], send_sem.at[1], recv_sem.at[1], local_sem)
    settle(1, out_ref)


def exchange_parts(parts, router, sizes, cid):
    n, high, lanes = parts.shape
    ways = router.shape[0] // n
    vm = pl.BlockSpec(memory_space=pltpu.VMEM)
    return pl.pallas_call(
        functools.partial(parts_kernel, sizes),
        out_shape=jax.ShapeDtypeStruct((n, ways, high, lanes), BF16),
        in_specs=[vm, vm], out_specs=vm,
        scratch_shapes=[
            pltpu.VMEM((n, high, lanes), BF16), pltpu.VMEM((n * high, lanes), F32),
            pltpu.VMEM((ways * n * high, lanes), F32), pltpu.VMEM((n, ways, high, lanes), BF16),
            pltpu.SemaphoreType.DMA((2,)), pltpu.SemaphoreType.DMA((2,)), pltpu.SemaphoreType.DMA],
        compiler_params=pltpu.CompilerParams(collective_id=cid, has_side_effects=True),
    )(parts, router)


def gram_kernel(rows_ref, gate_ref, up_ref, out_ref):
    step = pl.program_id(0)

    @pl.when(step == 0)
    def _():
        out_ref[...] = jnp.zeros_like(out_ref)

    rows = rows_ref[...]
    gate = dot(rows, gate_ref[...])
    upward = dot(rows, up_ref[...])
    hidden = (gate / (1.0 + jnp.exp(-gate)) * upward).astype(BF16)
    for b, (i, j) in enumerate(BLOCKS):
        left = hidden[:, i * LANES : (i + 1) * LANES]
        right = hidden[:, j * LANES : (j + 1) * LANES]
        out_ref[:, b * LANES : (b + 1) * LANES] += dot(left, right, ((0,), (0,)))

    @pl.when(step == pl.num_programs(0) - 1)
    def _():
        eye = (
            lax.broadcasted_iota(jnp.int32, (LANES, LANES), 0)
            == lax.broadcasted_iota(jnp.int32, (LANES, LANES), 1)
        ).astype(F32)
        for b, (i, j) in enumerate(BLOCKS):
            if i == j:
                out_ref[:, b * LANES : (b + 1) * LANES] += ridge_weight * eye


def packed_gram(rows, gate, up, tile=512):
    count, width = rows.shape
    hidden_units = gate.shape[1]
    return pl.pallas_call(
        gram_kernel,
        out_shape=jax.ShapeDtypeStruct((LANES, len(BLOCKS) * LANES), F32),
        grid=(count // tile,),
        in_specs=[
            pl.BlockSpec((tile, width), lambda s: (s, 0)),
            pl.BlockSpec((width, hidden_units), lambda s: (0, 0)),
            pl.BlockSpec((width, hidden_units), lambda s: (0, 0)),
        ],
        out_specs=pl.BlockSpec((LANES, len(BLOCKS) * LANES), lambda s: (0, 0)),
    )(rows, gate, up)


def inverse(block):
    size = block.shape[0]
    groups = size // 8
    lanes = lax.broadcasted_iota(jnp.int32, (8, size), 1)
    subs = lax.broadcasted_iota(jnp.int32, (8, size), 0)
    parts = [block[8 * g : 8 * g + 8, :] for g in range(groups)]
    for k in range(size):
        own, row = k // 8, k % 8
        pivot_row = jnp.broadcast_to(parts[own][row : row + 1, :], (8, size))
        pivot = jnp.broadcast_to(pivot_row[:, k : k + 1], (8, size))
        scaled = jnp.where(lanes == k, 1.0, pivot_row) / pivot
        fresh = []
        for g in range(groups):
            column = jnp.broadcast_to(parts[g][:, k : k + 1], (8, size))
            part = jnp.where(lanes == k, 0.0, parts[g]) - column * scaled
            if g == own:
                part = jnp.where(subs == row, scaled, part)
            fresh.append(part)
        parts = fresh
    return jnp.concatenate(parts, axis=0)


def solve_kernel(sum_ref, own_ref, down_ref, out_ref, work_ref, right_ref):
    def block(ref, b):
        return ref[:, b * LANES : (b + 1) * LANES]

    a00, a10, a11, a20, a21, a22 = (block(sum_ref, b) for b in range(6))
    nt = ((1,), (1,))
    tn = ((0,), (0,))

    work_ref[0] = a00
    g = [block(own_ref, b) for b in range(6)]
    right_ref[0] = jnp.concatenate([g[0], g[1].T, g[3].T], axis=1)
    right_ref[1] = jnp.concatenate([g[1], g[2], g[4].T], axis=1)
    right_ref[2] = jnp.concatenate([g[3], g[4], g[5]], axis=1)

    d0 = inverse(work_ref[0])
    l10 = dot(a10, d0, precision=HI)
    l20 = dot(a20, d0, precision=HI)
    a11 = a11 - dot(l10, a10, nt, precision=HI)
    a21 = a21 - dot(l20, a10, nt, precision=HI)
    a22 = a22 - dot(l20, a20, nt, precision=HI)
    d1 = inverse(a11)
    l21 = dot(a21, d1, precision=HI)
    a22 = a22 - dot(l21, a21, nt, precision=HI)
    d2 = inverse(a22)

    y0 = right_ref[0]
    y1 = right_ref[1] - dot(l10, y0, precision=HI)
    y2 = right_ref[2] - dot(l20, y0, precision=HI) - dot(l21, y1, precision=HI)
    x2 = dot(d2, y2, precision=HI)
    x1 = dot(d1, y1, precision=HI) - dot(l21, x2, tn, precision=HI)
    x0 = (
        dot(d0, y0, precision=HI)
        - dot(l10, x1, tn, precision=HI)
        - dot(l20, x2, tn, precision=HI)
    )
    for i, x in enumerate((x0, x1, x2)):
        high = x.astype(BF16)
        low = (x - high.astype(F32)).astype(BF16)
        down = down_ref[...]
        out_ref[i * LANES : (i + 1) * LANES, :] = (dot(high, down) + dot(low, down)).astype(BF16)


def member_part(gram_sum, gram_own, down):
    rows, width = down.shape
    return pl.pallas_call(
        solve_kernel,
        out_shape=jax.ShapeDtypeStruct((rows, width), BF16),
        scratch_shapes=[
            pltpu.VMEM((1, LANES, LANES), F32),
            pltpu.VMEM((3, LANES, 3 * LANES), F32),
        ],
    )(gram_sum, gram_own, down)


def cluster_slots(owners):
    count = owners.shape[0]
    same_owner = owners[:, None] == owners[None, :]
    earlier = lax.broadcasted_iota(jnp.int32, (count, count), 1) < lax.broadcasted_iota(
        jnp.int32, (count, count), 0
    )
    ranking = jnp.sum((same_owner & earlier).astype(jnp.int32), axis=1)
    return owners * OWN + ranking


def body(tokens, routing, gate_weight, up_weight, down_weight, cluster_of, owners):
    ys, zs, cores = (lax.axis_size(a) for a in SEQ)
    seq_count = ys * zs * cores
    rows_dev, width = tokens.shape
    topk = routing.shape[1]
    experts = cluster_of.shape[0]
    clusters = owners.shape[0]
    hidden_units = gate_weight.shape[2]
    capacity = min(rows_dev, max(2, 2 * rows_dev * topk // experts))
    out_width = down_weight.shape[2]

    slots = cluster_slots(owners)
    member_match = cluster_of[:, None] == lax.broadcasted_iota(jnp.int32, (experts, clusters), 1)
    member_slot = jnp.sum(jnp.where(member_match, slots[None, :], 0), axis=1)
    same_cluster = (cluster_of[:, None] == cluster_of[None, :]).astype(F32)
    slot_range = lax.broadcasted_iota(jnp.int32, (seq_count * OWN, experts), 0)
    route_owner = (slot_range == member_slot[None, :]).astype(F32)

    sizes = (ys, zs, cores)
    arrived = spread_tokens(tokens, routing.T, sizes, capacity, 0).reshape(-1, width)

    own_gram = packed_gram(arrived, gate_weight[0], up_weight[0])
    gram_sum = exchange_grams(own_gram, same_cluster, sizes, 1)
    part = member_part(gram_sum, own_gram, down_weight[0])

    wide = out_width // LANES
    high = hidden_units * wide // seq_count
    tall = hidden_units // high
    chunks = part.reshape(tall, high, wide, LANES).transpose(0, 2, 1, 3)
    chunks = chunks.reshape(seq_count, high, LANES)
    router = jnp.stack([same_cluster, route_owner], axis=1).astype(BF16)
    merged = exchange_parts(chunks, router.reshape(-1, experts), sizes, 2)
    merged = merged.reshape(tall, wide, 2, high, LANES).transpose(2, 0, 3, 1, 4)
    merged = merged.reshape(2, 1, hidden_units, out_width)
    differences = (merged[0].astype(F32) - down_weight.astype(F32)).astype(BF16)
    return (differences, merged[1])


def solution(mesh):
    finer = Mesh(
        mesh.devices.reshape(4, 16, 2, mesh.shape["layer"]), ("seq_0", "seq_1", "seq_2", "layer")
    )
    return jax.shard_map(
        body,
        mesh=finer,
        in_specs=(
            P(LAYER_SEQ, None),
            P(LAYER_SEQ, None),
            P(LAYER_SEQ, None, None),
            P(LAYER_SEQ, None, None),
            P(LAYER_SEQ, None, None),
            P("layer"),
            P("layer"),
        ),
        out_specs=(P(LAYER_SEQ, None, None), P(LAYER_SEQ, None, None)),
        check_vma=False,
    )
```

```python
import functools

import jax
import jax.numpy as jnp
from jax import lax
from jax.experimental import pallas as pl
from jax.experimental.pallas import tpu as pltpu
from jax.sharding import Mesh
from jax.sharding import PartitionSpec as P

OWN = 1
SEQ = ("seq_0", "seq_1", "seq_2")
PLANE = ("seq_0", "seq_2")
LAYER_SEQ = ("layer", "seq_0", "seq_1", "seq_2")
HI = lax.Precision.HIGHEST
F32 = jnp.float32
BF16 = jnp.bfloat16
MESH = pl.DeviceIdType.MESH

ridge_weight = 32.0
LANES = 128
BLOCKS = ((0, 0), (1, 0), (1, 1), (2, 0), (2, 1), (2, 2))


def dot(a, b, dims=((1,), (0,)), precision=None):
    return lax.dot_general(a, b, (dims, ((), ())), preferred_element_type=F32, precision=precision)


def tokens_kernel(sizes, tokens_ref, routing_ref, out_ref, held, ids, stage,
                  tok_send, tok_recv, ids_send, ids_recv, plane_send, plane_recv):
    ys, zs, cores = sizes
    rows = tokens_ref.shape[0]
    count, blocks, capacity, width = out_ref.shape
    halves = 2
    half = rows // halves
    y, z, c = (lax.axis_index(a) for a in SEQ)
    right, left = lax.rem(z + 1, zs), lax.rem(z + zs - 1, zs)
    peers = []
    for p in range(1, count):
        peers.append({"seq_0": lax.rem(y + p // cores, ys), "seq_2": lax.rem(c + p % cores, cores)})

    barrier = pltpu.get_barrier_semaphore()
    for target in [{"seq_1": right}, {"seq_1": left}] + peers:
        pl.semaphore_signal(barrier, inc=1, device_id=target, device_id_type=MESH)

    place = lax.broadcasted_iota(jnp.int32, (count, rows), 0)
    experts = (
        lax.rem(y + place // cores, ys) * (zs * cores) + z * cores + lax.rem(c + lax.rem(place, cores), cores)
    )
    upper = (
        lax.broadcasted_iota(jnp.int32, (rows, rows), 0)
        < lax.broadcasted_iota(jnp.int32, (rows, rows), 1)
    ).astype(BF16)
    slot_of = lax.broadcasted_iota(jnp.int32, (capacity, rows), 0).astype(F32)

    def token_copy(source, slot, part, target):
        rng = pl.ds(part * half, half)
        return pltpu.make_async_remote_copy(
            src_ref=source.at[rng, :], dst_ref=held.at[slot, rng, :],
            send_sem=tok_send.at[slot, part], recv_sem=tok_recv.at[slot, part],
            device_id={"seq_1": target}, device_id_type=MESH)

    def ids_copy(source, slot, target):
        return pltpu.make_async_remote_copy(
            src_ref=source, dst_ref=ids.at[slot],
            send_sem=ids_send.at[slot], recv_sem=ids_recv.at[slot],
            device_id={"seq_1": target}, device_id_type=MESH)

    def plane_copy(slot, p):
        return pltpu.make_async_remote_copy(
            src_ref=stage.at[slot, p - 1], dst_ref=out_ref.at[p, slot],
            send_sem=plane_send.at[p], recv_sem=plane_recv.at[p],
            device_id=peers[p - 1], device_id_type=MESH)

    def choose(slot, tokens, names):
        named = jnp.zeros((count, rows), F32)
        for k in range(names.shape[0]):
            named += (names[k : k + 1, :] == experts).astype(F32)
        before = dot(named.astype(BF16), upper)
        where = jnp.where(named > 0.0, before, -1.0)
        picker = jnp.concatenate(
            [(where[p : p + 1, :] == slot_of).astype(BF16) for p in range(count)], axis=0)
        chosen = dot(picker, tokens).astype(BF16)
        out_ref[0, slot] = chosen[:capacity]
        for p in range(1, count):
            stage[slot, p - 1] = chosen[p * capacity : (p + 1) * capacity]
        for p in range(1, count):
            plane_copy(slot, p).start()

    pl.semaphore_wait(barrier, count + 1)
    ups = zs // 2
    for part in range(halves):
        token_copy(tokens_ref, 1, part, right).start()
        token_copy(tokens_ref, zs - 1, part, left).start()
    ids_copy(routing_ref, 1, right).start()
    ids_copy(routing_ref, zs - 1, left).start()
    choose(0, tokens_ref[...], routing_ref[...])

    def take(slot, onward, target, last):
        ids_copy(ids.at[slot], slot, target).wait_recv()
        if not last:
            ids_copy(ids.at[slot], onward, target).start()
        for part in range(halves):
            token_copy(held.at[slot], slot, part, target).wait_recv()
            if not last:
                token_copy(held.at[slot], onward, part, target).start()

    def step(d, _):
        take(d, d + 1, right, False)
        take(zs - d, zs - d - 1, left, False)
        choose(d, held[d], ids[d])
        choose(zs - d, held[zs - d], ids[zs - d])
        return 0

    lax.fori_loop(1, ups - 1, step, 0)
    take(ups - 1, ups, right, False)
    take(ups + 1, ups, left, True)
    choose(ups - 1, held[ups - 1], ids[ups - 1])
    choose(ups + 1, held[ups + 1], ids[ups + 1])
    take(ups, 0, right, True)
    choose(ups, held[ups], ids[ups])

    def sent(slot, _):
        for part in range(halves):
            token_copy(tokens_ref, slot, part, right).wait_send()
        ids_copy(routing_ref, slot, right).wait_send()
        return 0

    lax.fori_loop(1, zs, sent, 0)
    for p in range(1, count):
        whole = pltpu.make_async_remote_copy(
            src_ref=out_ref.at[p], dst_ref=out_ref.at[p],
            send_sem=plane_send.at[p], recv_sem=plane_recv.at[p],
            device_id=peers[p - 1], device_id_type=MESH)
        whole.wait()


def spread_tokens(tokens, routing_t, sizes, capacity, cid):
    ys, zs, cores = sizes
    rows, width = tokens.shape
    count = ys * cores
    vm = pl.BlockSpec(memory_space=pltpu.VMEM)
    return pl.pallas_call(
        functools.partial(tokens_kernel, sizes),
        out_shape=jax.ShapeDtypeStruct((count, zs, capacity, width), BF16),
        in_specs=[vm, vm], out_specs=vm,
        scratch_shapes=[
            pltpu.VMEM((zs, rows, width), BF16),
            pltpu.VMEM((zs,) + routing_t.shape, jnp.int32),
            pltpu.VMEM((zs, count - 1, capacity, width), BF16),
            pltpu.SemaphoreType.DMA((zs, 2)), pltpu.SemaphoreType.DMA((zs, 2)),
            pltpu.SemaphoreType.DMA((zs,)), pltpu.SemaphoreType.DMA((zs,)),
            pltpu.SemaphoreType.DMA((count,)), pltpu.SemaphoreType.DMA((count,)),
        ],
        compiler_params=pltpu.CompilerParams(collective_id=cid, has_side_effects=True),
    )(tokens, routing_t)


def partner(i, sizes, here, sign):
    ys, zs, cores = sizes
    y, z, c = here
    dc = lax.rem(i, cores)
    rest = i // cores
    dy = lax.rem(rest, ys)
    zi = rest // ys
    dz = lax.rem(lax.rem(zi, 2) * ((zi + 1) // 2) + (1 - lax.rem(zi, 2)) * (zs - zi // 2), zs)
    if sign > 0:
        to = (lax.rem(y + dy, ys), lax.rem(z + dz, zs), lax.rem(c + dc, cores))
    else:
        to = (lax.rem(y + ys - dy, ys), lax.rem(z + zs - dz, zs), lax.rem(c + cores - dc, cores))
    return to, dict(zip(SEQ, to)), (to[0] * zs + to[1]) * cores + to[2]


def inverse(block, pivots=4):
    size = block.shape[0]
    lanes = lax.broadcasted_iota(jnp.int32, (8, size), 1)
    all_lanes = lax.broadcasted_iota(jnp.int32, (size, size), 1)
    subs = lax.broadcasted_iota(jnp.int32, (8, size), 0)

    def spread(x):
        return jnp.broadcast_to(x, (8, size))

    for k in range(0, size, pivots):
        own, row = 8 * (k // 8), k % 8
        rows = block[own : own + 8]
        mine = [spread(rows[:, k + j : k + j + 1]) for j in range(pivots)]
        inside = (lanes >= k) & (lanes < k + pivots)
        y = [
            jnp.where(
                lanes == k + j, 1.0, jnp.where(inside, 0.0, spread(rows[row + j : row + j + 1]))
            )
            for j in range(pivots)
        ]
        a = [[None] * pivots for _ in range(pivots)]
        for i in range(pivots):
            for j in range(i, pivots):
                a[i][j] = spread(mine[j][row + i : row + i + 1])
        d = [None] * pivots
        low = [[None] * pivots for _ in range(pivots)]
        for i in range(pivots):
            d[i] = 1.0 / a[i][i]
            for j in range(i + 1, pivots):
                low[j][i] = a[i][j] * d[i]
            for j in range(i + 1, pivots):
                for m in range(j, pivots):
                    a[j][m] = a[j][m] - low[j][i] * a[i][m]
                y[j] = y[j] - low[j][i] * y[i]
        y = [y[i] * d[i] for i in range(pivots)]
        for i in range(pivots - 1, -1, -1):
            for j in range(i):
                y[j] = y[j] - low[i][j] * y[i]
        fresh = jnp.where((all_lanes >= k) & (all_lanes < k + pivots), 0.0, block)
        for j in range(pivots):
            fresh = fresh - block[:, k + j : k + j + 1] * y[j][:1]
        fixed = fresh[own : own + 8]
        for j in range(pivots):
            fixed = jnp.where(subs == row + j, y[j], fixed)
        pieces = [fresh[:own], fixed, fresh[own + 8 :]]
        block = jnp.concatenate([p for p in pieces if p.shape[0]], axis=0)
    return block


def fill(ref, blocks):
    for b, (i, j) in enumerate(BLOCKS):
        x = blocks[b]
        ref[i * LANES : (i + 1) * LANES, j * LANES : (j + 1) * LANES] = x
        if i != j:
            ref[j * LANES : (j + 1) * LANES, i * LANES : (i + 1) * LANES] = x.T


def invert(ref):
    size = ref.shape[0]
    lanes = lax.broadcasted_iota(jnp.int32, (LANES, size), 1)
    all_lanes = lax.broadcasted_iota(jnp.int32, (size, size), 1)

    def stage(s, _):
        start = pl.multiple_of(s * LANES, LANES)
        own = pl.ds(start, LANES)
        pivot = inverse(ref[own, own])
        column = ref[:, own]
        across = dot(pivot, ref[own, :], precision=HI)
        inside = (lanes >= start) & (lanes < start + LANES)
        across = jnp.where(inside, jnp.concatenate([pivot] * (size // LANES), axis=1), across)
        inside = (all_lanes >= start) & (all_lanes < start + LANES)
        ref[...] = jnp.where(inside, 0.0, ref[...]) - dot(column, across, precision=HI)
        ref[own, :] = across
        return 0

    lax.fori_loop(0, size // LANES, stage, 0)


def merge_kernel(sizes, cuts, rows_ref, gate_ref, up_ref, down_ref, same_ref, router_ref,
                 diff_ref, slot_ref, gram, full, whole, g_out, g_in, s_out, s_in,
                 m_out, m_in, wide, mixed, b_out, b_in,
                 g_sems, s_sems, m_sems, b_sems, local_sem):
    n = sizes[0] * sizes[1] * sizes[2]
    here = tuple(lax.axis_index(x) for x in SEQ)
    me = (here[0] * sizes[1] + here[1]) * sizes[2] + here[2]
    barrier = pltpu.get_barrier_semaphore()
    blocks = len(BLOCKS)
    per = blocks // cuts
    size = full.shape[0]
    width = down_ref.shape[1]
    wide_groups = width // LANES
    parts = size // LANES
    tall = LANES // 8

    def hello(i, _):
        _, to, _ = partner(i, sizes, here, 1)
        pl.semaphore_signal(barrier, inc=1, device_id=to, device_id_type=MESH)
        return 0

    lax.fori_loop(1, n, hello, 0)

    gram[...] = jnp.zeros_like(gram)
    tile = 512

    def accumulate(s, _):
        rows = rows_ref[pl.ds(pl.multiple_of(s * tile, tile), tile), :]
        gate = dot(rows, gate_ref[...])
        upward = dot(rows, up_ref[...])
        hidden = (gate / (1.0 + jnp.exp(-gate)) * upward).astype(BF16)
        for b, (i, j) in enumerate(BLOCKS):
            left = hidden[:, i * LANES : (i + 1) * LANES]
            right = hidden[:, j * LANES : (j + 1) * LANES]
            gram[:, b * LANES : (b + 1) * LANES] += dot(left, right, ((0,), (0,)))
        return 0

    lax.fori_loop(0, rows_ref.shape[0] // tile, accumulate, 0)
    eye = (
        lax.broadcasted_iota(jnp.int32, (LANES, LANES), 0)
        == lax.broadcasted_iota(jnp.int32, (LANES, LANES), 1)
    ).astype(F32)
    for b, (i, j) in enumerate(BLOCKS):
        if i == j:
            gram[:, b * LANES : (b + 1) * LANES] += ridge_weight * eye
        h, k = b // per, b % per
        g_out[h, pl.ds(k, n, stride=8), :] = gram[:, b * LANES : (b + 1) * LANES]

    pl.semaphore_wait(barrier, n - 1)

    def send(src, dst, sems, h):
        own = pltpu.make_async_copy(src(me), dst(me), local_sem)
        own.start()

        def one(i, _):
            _, to, index = partner(i, sizes, here, 1)
            pltpu.make_async_remote_copy(
                src_ref=src(index), dst_ref=dst(me), send_sem=sems.at[0, h], recv_sem=sems.at[1, h],
                device_id=to, device_id_type=MESH).start()
            return 0

        lax.fori_loop(1, n, one, 0)
        own.wait()

    def settle(ref, sems, h):
        pltpu.make_async_remote_copy(
            src_ref=ref, dst_ref=ref, send_sem=sems.at[0, h], recv_sem=sems.at[1, h],
            device_id={"seq_0": 0}, device_id_type=MESH).wait()

    def lines(ref, h):
        return lambda i: ref.at[h, pl.ds(pl.multiple_of(i * 8, 8), per), :]

    def settle_lines(ref, sems, h):
        settle(ref.at[h, pl.ds(0, (n - 1) * per), :], sems, h)

    for h in range(cuts):
        send(lines(g_out, h), lines(g_in, h), g_sems, h)
    fill(whole, [gram[:, b * LANES : (b + 1) * LANES] for b in range(blocks)])
    same = same_ref[...]
    for h in range(cuts):
        settle_lines(g_in, g_sems, h)
        for k in range(per):
            s_out[h, pl.ds(k, n, stride=8), :] = dot(
                same, g_in[h, pl.ds(k, n, stride=8), :], precision=HI)
        send(lines(s_out, h), lines(s_in, h), s_sems, h)
    for h in range(cuts):
        settle_lines(s_in, s_sems, h)
    fill(full, [s_in[b // per, pl.ds(b % per, n, stride=8), :] for b in range(blocks)])
    invert(full)

    for p in range(parts):
        x = dot(full[p * LANES : (p + 1) * LANES, :], whole[...], precision=HI)
        high = x.astype(BF16)
        low = (x - high.astype(F32)).astype(BF16)
        down = down_ref[...]
        part = dot(high, down) + dot(low, down)
        for g in range(tall):
            for c in range(wide_groups):
                m_out[p, g * wide_groups + c] = part[
                    g * 8 : g * 8 + 8, c * LANES : (c + 1) * LANES].astype(BF16)
        send(lambda i: m_out.at[p, i], lambda i: m_in.at[p, i], m_sems, p)

    router = router_ref[...]
    ways = router.shape[0] // n
    for p in range(parts):
        settle(m_in.at[p, pl.ds(0, n - 1)], m_sems, p)

        def widen(i, _):
            wide[pl.ds(pl.multiple_of(i * 8, 8), 8), :] = m_in[p, i].astype(F32)
            return 0

        lax.fori_loop(0, n, widen, 0, unroll=8)

        def mix(r, _):
            x = wide[pl.ds(r, n, stride=8), :].astype(BF16)
            mixed[pl.ds(r, ways * n, stride=8), :] = dot(router, x)
            return 0

        lax.fori_loop(0, 8, mix, 0, unroll=4)

        def narrow(i, _):
            for w in range(ways):
                b_out[p, i, w] = mixed[pl.ds(pl.multiple_of((i * ways + w) * 8, 8), 8), :].astype(BF16)
            return 0

        lax.fori_loop(0, n, narrow, 0, unroll=4)
        send(lambda i: b_out.at[p, i], lambda i: b_in.at[p, i], b_sems, p)

    for p in range(parts):
        settle(b_in.at[p, pl.ds(0, n - 1)], b_sems, p)

        def finish(g, _):
            rows = pl.ds(pl.multiple_of(p * LANES + g * 16, 16), 16)
            for c in range(wide_groups):
                columns = slice(c * LANES, (c + 1) * LANES)
                upper = g * 2 * wide_groups + c
                mine, held = (
                    jnp.concatenate(
                        [b_in[p, upper, w].astype(F32), b_in[p, upper + wide_groups, w].astype(F32)],
                        axis=0)
                    for w in range(ways)
                )
                diff_ref[rows, columns] = (mine - down_ref[rows, columns].astype(F32)).astype(BF16)
                slot_ref[rows, columns] = held.astype(BF16)
            return 0

        lax.fori_loop(0, LANES // 16, finish, 0)


def merge(rows, gate, up, down, same, router, sizes, cid, cuts=2):
    n = sizes[0] * sizes[1] * sizes[2]
    size, width = down.shape
    parts = size // LANES
    ways = router.shape[0] // n
    blocks = len(BLOCKS)
    vm = pl.BlockSpec(memory_space=pltpu.VMEM)
    lines = pltpu.VMEM((cuts, n * 8, LANES), F32)
    dma = pltpu.SemaphoreType.DMA
    return pl.pallas_call(
        functools.partial(merge_kernel, sizes, cuts),
        out_shape=(jax.ShapeDtypeStruct((size, width), BF16),) * 2,
        in_specs=[vm] * 6,
        out_specs=(vm, vm),
        scratch_shapes=[
            pltpu.VMEM((LANES, blocks * LANES), F32),
            pltpu.VMEM((size, size), F32),
            pltpu.VMEM((size, size), F32),
            lines, lines, lines, lines,
            pltpu.VMEM((parts, n, 8, LANES), BF16),
            pltpu.VMEM((parts, n, 8, LANES), BF16),
            pltpu.VMEM((n * 8, LANES), F32),
            pltpu.VMEM((ways * n * 8, LANES), F32),
            pltpu.VMEM((parts, n, ways, 8, LANES), BF16),
            pltpu.VMEM((parts, n, ways, 8, LANES), BF16),
            dma((2, cuts)), dma((2, cuts)), dma((2, parts)), dma((2, parts)), dma,
        ],
        compiler_params=pltpu.CompilerParams(collective_id=cid, has_side_effects=True),
    )(rows, gate, up, down, same, router)


def cluster_slots(owners):
    count = owners.shape[0]
    same_owner = owners[:, None] == owners[None, :]
    earlier = lax.broadcasted_iota(jnp.int32, (count, count), 1) < lax.broadcasted_iota(
        jnp.int32, (count, count), 0
    )
    ranking = jnp.sum((same_owner & earlier).astype(jnp.int32), axis=1)
    return owners * OWN + ranking


def body(tokens, routing, gate_weight, up_weight, down_weight, cluster_of, owners):
    ys, zs, cores = (lax.axis_size(a) for a in SEQ)
    seq_count = ys * zs * cores
    rows_dev, width = tokens.shape
    topk = routing.shape[1]
    experts = cluster_of.shape[0]
    clusters = owners.shape[0]
    capacity = min(rows_dev, max(2, 2 * rows_dev * topk // experts))

    slots = cluster_slots(owners)
    member_match = cluster_of[:, None] == lax.broadcasted_iota(jnp.int32, (experts, clusters), 1)
    member_slot = jnp.sum(jnp.where(member_match, slots[None, :], 0), axis=1)
    same_cluster = (cluster_of[:, None] == cluster_of[None, :]).astype(F32)
    slot_range = lax.broadcasted_iota(jnp.int32, (seq_count * OWN, experts), 0)
    route_owner = (slot_range == member_slot[None, :]).astype(F32)

    sizes = (ys, zs, cores)
    arrived = spread_tokens(tokens, routing.T, sizes, capacity, 0).reshape(-1, width)

    router = jnp.stack([same_cluster, route_owner], axis=1).astype(BF16)
    differences, merged_slots = merge(
        arrived, gate_weight[0], up_weight[0], down_weight[0], same_cluster,
        router.reshape(-1, experts), sizes, 1)
    return (differences[None], merged_slots[None])


def solution(mesh):
    finer = Mesh(
        mesh.devices.reshape(4, 16, 2, mesh.shape["layer"]), ("seq_0", "seq_1", "seq_2", "layer")
    )
    return jax.shard_map(
        body,
        mesh=finer,
        in_specs=(
            P(LAYER_SEQ, None),
            P(LAYER_SEQ, None),
            P(LAYER_SEQ, None, None),
            P(LAYER_SEQ, None, None),
            P(LAYER_SEQ, None, None),
            P("layer"),
            P("layer"),
        ),
        out_specs=(P(LAYER_SEQ, None, None), P(LAYER_SEQ, None, None)),
        check_vma=False,
    )
```

```python
import functools

import jax
import jax.numpy as jnp
from jax import lax
from jax.experimental import pallas as pl
from jax.experimental.pallas import tpu as pltpu
from jax.sharding import Mesh
from jax.sharding import PartitionSpec as P

OWN = 1
SEQ = ("seq_0", "seq_1", "seq_2")
PLANE = ("seq_0", "seq_2")
LAYER_SEQ = ("layer", "seq_0", "seq_1", "seq_2")
HI = lax.Precision.HIGHEST
F32 = jnp.float32
BF16 = jnp.bfloat16
MESH = pl.DeviceIdType.MESH

ridge_weight = 32.0
LANES = 128
BLOCKS = ((0, 0), (1, 0), (1, 1), (2, 0), (2, 1), (2, 2))


def dot(a, b, dims=((1,), (0,)), precision=None):
    return lax.dot_general(a, b, (dims, ((), ())), preferred_element_type=F32, precision=precision)


def tokens_kernel(sizes, tokens_ref, routing_ref, out_ref, held, ids, stage,
                  tok_send, tok_recv, ids_send, ids_recv, plane_send, plane_recv):
    ys, zs, cores = sizes
    rows = tokens_ref.shape[0]
    count, blocks, capacity, width = out_ref.shape
    halves = 2
    half = rows // halves
    y, z, c = (lax.axis_index(a) for a in SEQ)
    right, left = lax.rem(z + 1, zs), lax.rem(z + zs - 1, zs)
    peers = []
    for p in range(1, count):
        peers.append({"seq_0": lax.rem(y + p // cores, ys), "seq_2": lax.rem(c + p % cores, cores)})

    barrier = pltpu.get_barrier_semaphore()
    for target in [{"seq_1": right}, {"seq_1": left}] + peers:
        pl.semaphore_signal(barrier, inc=1, device_id=target, device_id_type=MESH)

    place = lax.broadcasted_iota(jnp.int32, (count, rows), 0)
    experts = (
        lax.rem(y + place // cores, ys) * (zs * cores) + z * cores + lax.rem(c + lax.rem(place, cores), cores)
    )
    upper = (
        lax.broadcasted_iota(jnp.int32, (rows, rows), 0)
        < lax.broadcasted_iota(jnp.int32, (rows, rows), 1)
    ).astype(BF16)
    slot_of = lax.broadcasted_iota(jnp.int32, (capacity, rows), 0).astype(F32)

    def token_copy(source, slot, part, target):
        rng = pl.ds(part * half, half)
        return pltpu.make_async_remote_copy(
            src_ref=source.at[rng, :], dst_ref=held.at[slot, rng, :],
            send_sem=tok_send.at[slot, part], recv_sem=tok_recv.at[slot, part],
            device_id={"seq_1": target}, device_id_type=MESH)

    def ids_copy(source, slot, target):
        return pltpu.make_async_remote_copy(
            src_ref=source, dst_ref=ids.at[slot],
            send_sem=ids_send.at[slot], recv_sem=ids_recv.at[slot],
            device_id={"seq_1": target}, device_id_type=MESH)

    def plane_copy(slot, p):
        return pltpu.make_async_remote_copy(
            src_ref=stage.at[slot, p - 1], dst_ref=out_ref.at[p, slot],
            send_sem=plane_send.at[p], recv_sem=plane_recv.at[p],
            device_id=peers[p - 1], device_id_type=MESH)

    def choose(slot, tokens, names):
        named = jnp.zeros((count, rows), F32)
        for k in range(names.shape[0]):
            named += (names[k : k + 1, :] == experts).astype(F32)
        before = dot(named.astype(BF16), upper)
        where = jnp.where(named > 0.0, before, -1.0)
        picker = jnp.concatenate(
            [(where[p : p + 1, :] == slot_of).astype(BF16) for p in range(count)], axis=0
        )
        chosen = dot(picker, tokens).astype(BF16)
        out_ref[0, slot] = chosen[:capacity]
        for p in range(1, count):
            stage[slot, p - 1] = chosen[p * capacity : (p + 1) * capacity]
        for p in range(1, count):
            plane_copy(slot, p).start()

    pl.semaphore_wait(barrier, count + 1)
    ups = zs // 2
    ids_copy(routing_ref, 1, right).start()
    ids_copy(routing_ref, zs - 1, left).start()
    for part in range(halves):
        token_copy(tokens_ref, 1, part, right).start()
        token_copy(tokens_ref, zs - 1, part, left).start()

    def take(slot, part, onward, target):
        token_copy(held.at[slot], slot, part, target).wait_recv()
        if onward is not None:
            token_copy(held.at[slot], onward, part, target).start()

    def take_ids(slot, onward, target):
        ids_copy(ids.at[slot], slot, target).wait_recv()
        if onward is not None:
            ids_copy(ids.at[slot], onward, target).start()

    def lead(d):
        take_ids(d, d + 1, right)
        take(d, 0, d + 1, right)
        take_ids(zs - d, zs - d - 1, left)
        take(zs - d, 0, zs - d - 1, left)

    def follow(d):
        take(d, 1, d + 1, right)
        take(zs - d, 1, zs - d - 1, left)

    lead(1)
    choose(0, tokens_ref[...], routing_ref[...])
    follow(1)

    def step(d, _):
        lead(d)
        choose(d - 1, held[d - 1], ids[d - 1])
        follow(d)
        choose(zs - d + 1, held[zs - d + 1], ids[zs - d + 1])
        return 0

    lax.fori_loop(2, ups - 1, step, 0)
    low, high = ups - 1, ups + 1
    take_ids(low, ups, right)
    take(low, 0, ups, right)
    take_ids(high, None, left)
    take(high, 0, None, left)
    choose(low - 1, held[low - 1], ids[low - 1])
    take(low, 1, None, right)
    take(high, 1, ups, left)
    choose(high + 1, held[high + 1], ids[high + 1])
    choose(low, held[low], ids[low])
    choose(high, held[high], ids[high])
    take_ids(ups, None, right)
    take(ups, 0, None, right)
    take(ups, 1, None, left)
    choose(ups, held[ups], ids[ups])

    def sent(slot, _):
        for part in range(halves):
            token_copy(tokens_ref, slot, part, right).wait_send()
        ids_copy(routing_ref, slot, right).wait_send()
        return 0

    lax.fori_loop(1, zs, sent, 0)
    for p in range(1, count):
        whole = pltpu.make_async_remote_copy(
            src_ref=out_ref.at[p], dst_ref=out_ref.at[p],
            send_sem=plane_send.at[p], recv_sem=plane_recv.at[p],
            device_id=peers[p - 1], device_id_type=MESH)
        whole.wait()


def spread_tokens(tokens, routing_t, sizes, capacity, cid):
    ys, zs, cores = sizes
    rows, width = tokens.shape
    count = ys * cores
    vm = pl.BlockSpec(memory_space=pltpu.VMEM)
    return pl.pallas_call(
        functools.partial(tokens_kernel, sizes),
        out_shape=jax.ShapeDtypeStruct((count, zs, capacity, width), BF16),
        in_specs=[vm, vm], out_specs=vm,
        scratch_shapes=[
            pltpu.VMEM((zs, rows, width), BF16),
            pltpu.VMEM((zs,) + routing_t.shape, jnp.int32),
            pltpu.VMEM((zs, count - 1, capacity, width), BF16),
            pltpu.SemaphoreType.DMA((zs, 2)), pltpu.SemaphoreType.DMA((zs, 2)),
            pltpu.SemaphoreType.DMA((zs,)), pltpu.SemaphoreType.DMA((zs,)),
            pltpu.SemaphoreType.DMA((count,)), pltpu.SemaphoreType.DMA((count,)),
        ],
        compiler_params=pltpu.CompilerParams(collective_id=cid, has_side_effects=True),
    )(tokens, routing_t)


def partner(i, sizes, here, sign):
    ys, zs, cores = sizes
    y, z, c = here
    dc = lax.rem(i, cores)
    rest = i // cores
    dy = lax.rem(rest, ys)
    zi = rest // ys
    dz = lax.rem(lax.rem(zi, 2) * ((zi + 1) // 2) + (1 - lax.rem(zi, 2)) * (zs - zi // 2), zs)
    if sign > 0:
        to = (lax.rem(y + dy, ys), lax.rem(z + dz, zs), lax.rem(c + dc, cores))
    else:
        to = (lax.rem(y + ys - dy, ys), lax.rem(z + zs - dz, zs), lax.rem(c + cores - dc, cores))
    return to, dict(zip(SEQ, to)), (to[0] * zs + to[1]) * cores + to[2]


def inverse(block, pivots=4):
    size = block.shape[0]
    lanes = lax.broadcasted_iota(jnp.int32, (8, size), 1)
    all_lanes = lax.broadcasted_iota(jnp.int32, (size, size), 1)
    subs = lax.broadcasted_iota(jnp.int32, (8, size), 0)

    def spread(x):
        return jnp.broadcast_to(x, (8, size))

    for k in range(0, size, pivots):
        own, row = 8 * (k // 8), k % 8
        rows = block[own : own + 8]
        mine = [spread(rows[:, k + j : k + j + 1]) for j in range(pivots)]
        inside = (lanes >= k) & (lanes < k + pivots)
        y = [
            jnp.where(
                lanes == k + j, 1.0, jnp.where(inside, 0.0, spread(rows[row + j : row + j + 1]))
            )
            for j in range(pivots)
        ]
        a = [[None] * pivots for _ in range(pivots)]
        for i in range(pivots):
            for j in range(i, pivots):
                a[i][j] = spread(mine[j][row + i : row + i + 1])
        d = [None] * pivots
        low = [[None] * pivots for _ in range(pivots)]
        for i in range(pivots):
            d[i] = 1.0 / a[i][i]
            for j in range(i + 1, pivots):
                low[j][i] = a[i][j] * d[i]
            for j in range(i + 1, pivots):
                for m in range(j, pivots):
                    a[j][m] = a[j][m] - low[j][i] * a[i][m]
                y[j] = y[j] - low[j][i] * y[i]
        y = [y[i] * d[i] for i in range(pivots)]
        for i in range(pivots - 1, -1, -1):
            for j in range(i):
                y[j] = y[j] - low[i][j] * y[i]
        fresh = jnp.where((all_lanes >= k) & (all_lanes < k + pivots), 0.0, block)
        for j in range(pivots):
            fresh = fresh - block[:, k + j : k + j + 1] * y[j][:1]
        fixed = fresh[own : own + 8]
        for j in range(pivots):
            fixed = jnp.where(subs == row + j, y[j], fixed)
        pieces = [fresh[:own], fixed, fresh[own + 8 :]]
        block = jnp.concatenate([p for p in pieces if p.shape[0]], axis=0)
    return block


def solve(a, right):
    nt, tn = ((1,), (1,)), ((0,), (0,))
    a00, a10, a11, a20, a21, a22 = a
    d0 = inverse(a00)
    l10 = dot(a10, d0, precision=HI)
    l20 = dot(a20, d0, precision=HI)
    a11 = a11 - dot(l10, a10, nt, precision=HI)
    d1 = inverse(a11)
    a21 = a21 - dot(l20, a10, nt, precision=HI)
    a22 = a22 - dot(l20, a20, nt, precision=HI)
    y1 = right[1] - dot(l10, right[0], precision=HI)
    z0 = dot(d0, right[0], precision=HI)
    l21 = dot(a21, d1, precision=HI)
    a22 = a22 - dot(l21, a21, nt, precision=HI)
    d2 = inverse(a22)
    y2 = right[2] - dot(l20, right[0], precision=HI) - dot(l21, y1, precision=HI)
    z1 = dot(d1, y1, precision=HI)
    x2 = dot(d2, y2, precision=HI)
    x1 = z1 - dot(l21, x2, tn, precision=HI)
    x0 = z0 - dot(l10, x1, tn, precision=HI) - dot(l20, x2, tn, precision=HI)
    return x0, x1, x2


def as_column(row, count, repeat=1):
    size = row.shape[1]
    shape = (count * repeat, size)
    hit = lax.broadcasted_iota(jnp.int32, shape, 0) // repeat == lax.broadcasted_iota(
        jnp.int32, shape, 1
    )
    return jnp.sum(jnp.where(hit, jnp.broadcast_to(row, shape), 0.0), axis=1, keepdims=True)


def tables(cluster_ref, owners_ref, ways):
    cluster = cluster_ref[...].astype(F32)
    owners = owners_ref[...].astype(F32)
    experts, clusters = cluster.shape[1], owners.shape[1]
    same = (as_column(cluster, experts) == cluster).astype(F32)

    owner = as_column(owners, clusters)
    square = (clusters, clusters)
    earlier = lax.broadcasted_iota(jnp.int32, square, 1) < lax.broadcasted_iota(jnp.int32, square, 0)
    ranking = jnp.sum(jnp.where((owner == owners) & earlier, 1.0, 0.0), axis=1, keepdims=True)
    slots = owner * OWN + ranking
    shape = (clusters, experts)
    member = lax.broadcasted_iota(jnp.int32, shape, 0).astype(F32) == cluster
    member_slot = jnp.sum(jnp.where(member, slots, 0.0), axis=0, keepdims=True)

    shape = (experts * ways, experts)
    row = lax.broadcasted_iota(jnp.int32, shape, 0)
    mine = as_column(cluster, experts, ways) == cluster
    held = member_slot == (row // ways).astype(F32)
    router = jnp.where(row % ways == 0, mine.astype(F32), held.astype(F32)).astype(BF16)
    return same, router


def merge_kernel(sizes, cuts, rows_ref, gate_ref, up_ref, down_ref, cluster_ref, owners_ref,
                 b_in, gram, whole, g_out, g_in, s_out, s_in,
                 m_out, m_in, wide, mixed, b_out,
                 g_sems, s_sems, m_sems, b_sems, local_sem):
    n = sizes[0] * sizes[1] * sizes[2]
    here = tuple(lax.axis_index(x) for x in SEQ)
    me = (here[0] * sizes[1] + here[1]) * sizes[2] + here[2]
    barrier = pltpu.get_barrier_semaphore()
    blocks = len(BLOCKS)
    per = blocks // cuts
    size, width = down_ref.shape
    wide_groups = width // LANES
    parts = size // LANES
    tall = LANES // 8

    def hello(i, _):
        _, to, _ = partner(i, sizes, here, 1)
        pl.semaphore_signal(barrier, inc=1, device_id=to, device_id_type=MESH)
        return 0

    lax.fori_loop(1, n, hello, 0)

    gram[...] = jnp.zeros_like(gram)
    tile = 512

    def accumulate(s, _):
        rows = rows_ref[pl.ds(pl.multiple_of(s * tile, tile), tile), :]
        gate = dot(rows, gate_ref[...])
        upward = dot(rows, up_ref[...])
        hidden = (gate / (1.0 + jnp.exp(-gate)) * upward).astype(BF16)
        for b, (i, j) in enumerate(BLOCKS):
            left = hidden[:, i * LANES : (i + 1) * LANES]
            right = hidden[:, j * LANES : (j + 1) * LANES]
            gram[:, b * LANES : (b + 1) * LANES] += dot(left, right, ((0,), (0,)))
        return 0

    lax.fori_loop(0, rows_ref.shape[0] // tile, accumulate, 0)
    eye = (
        lax.broadcasted_iota(jnp.int32, (LANES, LANES), 0)
        == lax.broadcasted_iota(jnp.int32, (LANES, LANES), 1)
    ).astype(F32)
    for b, (i, j) in enumerate(BLOCKS):
        if i == j:
            gram[:, b * LANES : (b + 1) * LANES] += ridge_weight * eye
        h, k = b // per, b % per
        g_out[h, pl.ds(k, n, stride=8), :] = gram[:, b * LANES : (b + 1) * LANES]

    pl.semaphore_wait(barrier, n - 1)

    def send(src, dst, sems, h):
        own = pltpu.make_async_copy(src(me), dst(me), local_sem)
        own.start()

        def one(i, _):
            _, to, index = partner(i, sizes, here, 1)
            pltpu.make_async_remote_copy(
                src_ref=src(index), dst_ref=dst(me), send_sem=sems.at[0, h], recv_sem=sems.at[1, h],
                device_id=to, device_id_type=MESH).start()
            return 0

        lax.fori_loop(1, n, one, 0)
        own.wait()

    def settle(ref, sems, h):
        pltpu.make_async_remote_copy(
            src_ref=ref, dst_ref=ref, send_sem=sems.at[0, h], recv_sem=sems.at[1, h],
            device_id={"seq_0": 0}, device_id_type=MESH).wait()

    def lines(ref, h):
        return lambda i: ref.at[h, pl.ds(pl.multiple_of(i * 8, 8), per), :]

    def settle_lines(ref, sems, h):
        settle(ref.at[h, pl.ds(0, (n - 1) * per), :], sems, h)

    for h in range(cuts):
        send(lines(g_out, h), lines(g_in, h), g_sems, h)

    ways = b_in.shape[2]
    same, router = tables(cluster_ref, owners_ref, ways)
    own = [gram[:, b * LANES : (b + 1) * LANES] for b in range(blocks)]
    whole[0] = jnp.concatenate([own[0], own[1].T, own[3].T], axis=1)
    whole[1] = jnp.concatenate([own[1], own[2], own[4].T], axis=1)
    whole[2] = jnp.concatenate([own[3], own[4], own[5]], axis=1)
    for h in range(cuts):
        settle_lines(g_in, g_sems, h)
        for k in range(per):
            s_out[h, pl.ds(k, n, stride=8), :] = dot(
                same, g_in[h, pl.ds(k, n, stride=8), :], precision=HI)
        send(lines(s_out, h), lines(s_in, h), s_sems, h)
    for h in range(cuts):
        settle_lines(s_in, s_sems, h)

    solved = solve(
        [s_in[b // per, pl.ds(b % per, n, stride=8), :] for b in range(blocks)],
        [whole[i] for i in range(parts)])
    down = down_ref[...]
    for p in range(parts):
        high = solved[p].astype(BF16)
        low = (solved[p] - high.astype(F32)).astype(BF16)
        part = dot(high, down) + dot(low, down)
        for g in range(tall):
            for c in range(wide_groups):
                m_out[p, g * wide_groups + c] = part[
                    g * 8 : g * 8 + 8, c * LANES : (c + 1) * LANES].astype(BF16)
        send(lambda i: m_out.at[p, i], lambda i: m_in.at[p, i], m_sems, p)

    for p in range(parts):
        settle(m_in.at[p, pl.ds(0, n - 1)], m_sems, p)

        def widen(i, _):
            wide[pl.ds(pl.multiple_of(i * 8, 8), 8), :] = m_in[p, i].astype(F32)
            return 0

        lax.fori_loop(0, n, widen, 0, unroll=8)

        def mix(r, _):
            x = wide[pl.ds(r, n, stride=8), :].astype(BF16)
            mixed[pl.ds(r, ways * n, stride=8), :] = dot(router, x)
            return 0

        lax.fori_loop(0, 8, mix, 0, unroll=4)

        def narrow(i, _):
            for w in range(ways):
                b_out[p, i, w] = mixed[pl.ds(pl.multiple_of((i * ways + w) * 8, 8), 8), :].astype(BF16)
            return 0

        lax.fori_loop(0, n, narrow, 0, unroll=4)
        send(lambda i: b_out.at[p, i], lambda i: b_in.at[p, i], b_sems, p)

    for p in range(parts):
        settle(b_in.at[p, pl.ds(0, n - 1)], b_sems, p)


def merge(rows, gate, up, down, cluster_of, owners, sizes, cid, cuts=2, ways=2):
    n = sizes[0] * sizes[1] * sizes[2]
    size, width = down.shape
    parts = size // LANES
    blocks = len(BLOCKS)
    vm = pl.BlockSpec(memory_space=pltpu.VMEM)
    lines = pltpu.VMEM((cuts, n * 8, LANES), F32)
    dma = pltpu.SemaphoreType.DMA
    return pl.pallas_call(
        functools.partial(merge_kernel, sizes, cuts),
        out_shape=jax.ShapeDtypeStruct((parts, n, ways, 8, LANES), BF16),
        in_specs=[vm] * 6,
        out_specs=vm,
        scratch_shapes=[
            pltpu.VMEM((LANES, blocks * LANES), F32),
            pltpu.VMEM((parts, LANES, size), F32),
            lines, lines, lines, lines,
            pltpu.VMEM((parts, n, 8, LANES), BF16),
            pltpu.VMEM((parts, n, 8, LANES), BF16),
            pltpu.VMEM((n * 8, LANES), F32),
            pltpu.VMEM((ways * n * 8, LANES), F32),
            pltpu.VMEM((parts, n, ways, 8, LANES), BF16),
            dma((2, cuts)), dma((2, cuts)), dma((2, parts)), dma((2, parts)), dma,
        ],
        compiler_params=pltpu.CompilerParams(collective_id=cid, has_side_effects=True),
    )(rows, gate, up, down, cluster_of.reshape(1, -1), owners.reshape(1, -1))


def finish_kernel(chunks_ref, down_ref, diff_ref, slot_ref):
    wide_groups = down_ref.shape[1] // LANES
    for g in range(down_ref.shape[0] // 16):
        rows = slice(g * 16, g * 16 + 16)
        for c in range(wide_groups):
            columns = slice(c * LANES, (c + 1) * LANES)
            upper = g * 2 * wide_groups + c
            mine, held = (
                jnp.concatenate(
                    [chunks_ref[0, upper, w], chunks_ref[0, upper + wide_groups, w]], axis=0)
                for w in range(2)
            )
            diff_ref[rows, columns] = (
                mine.astype(F32) - down_ref[rows, columns].astype(F32)
            ).astype(BF16)
            slot_ref[rows, columns] = held


def finish(chunks, down):
    size, width = down.shape
    block = pl.BlockSpec((LANES, width), lambda p: (p, 0))
    return pl.pallas_call(
        finish_kernel,
        out_shape=(jax.ShapeDtypeStruct((size, width), BF16),) * 2,
        grid=(chunks.shape[0],),
        in_specs=[pl.BlockSpec((1,) + chunks.shape[1:], lambda p: (p, 0, 0, 0, 0)), block],
        out_specs=(block, block),
    )(chunks, down)


def body(tokens, routing, gate_weight, up_weight, down_weight, cluster_of, owners):
    ys, zs, cores = (lax.axis_size(a) for a in SEQ)
    rows_dev, width = tokens.shape
    topk = routing.shape[1]
    experts = cluster_of.shape[0]
    capacity = min(rows_dev, max(2, 2 * rows_dev * topk // experts))

    sizes = (ys, zs, cores)
    arrived = spread_tokens(tokens, routing.T, sizes, capacity, 0).reshape(-1, width)

    chunks = merge(
        arrived, gate_weight[0], up_weight[0], down_weight[0], cluster_of, owners, sizes, 1)
    differences, merged_slots = finish(chunks, down_weight[0])
    return (differences[None], merged_slots[None])


def solution(mesh):
    finer = Mesh(
        mesh.devices.reshape(4, 16, 2, mesh.shape["layer"]), ("seq_0", "seq_1", "seq_2", "layer")
    )
    return jax.shard_map(
        body,
        mesh=finer,
        in_specs=(
            P(LAYER_SEQ, None),
            P(LAYER_SEQ, None),
            P(LAYER_SEQ, None, None),
            P(LAYER_SEQ, None, None),
            P(LAYER_SEQ, None, None),
            P("layer"),
            P("layer"),
        ),
        out_specs=(P(LAYER_SEQ, None, None), P(LAYER_SEQ, None, None)),
        check_vma=False,
    )
```

```python
import functools

import jax
import jax.numpy as jnp
from jax import lax
from jax.experimental import pallas as pl
from jax.experimental.pallas import tpu as pltpu
from jax.sharding import Mesh
from jax.sharding import PartitionSpec as P

OWN = 1
SEQ = ("seq_0", "seq_1", "seq_2")
PLANE = ("seq_0", "seq_2")
LAYER_SEQ = ("layer", "seq_0", "seq_1", "seq_2")
HI = lax.Precision.HIGHEST
F32 = jnp.float32
BF16 = jnp.bfloat16
MESH = pl.DeviceIdType.MESH

ridge_weight = 32.0
LANES = 128
BLOCKS = ((0, 0), (1, 0), (1, 1), (2, 0), (2, 1), (2, 2))


def dot(a, b, dims=((1,), (0,)), precision=None):
    return lax.dot_general(a, b, (dims, ((), ())), preferred_element_type=F32, precision=precision)


def gather_gram(sizes, tokens_ref, routing_ref, gate_ref, up_ref, gram, out_ref, held, ids, stage,
                tok_send, tok_recv, ids_send, ids_recv, plane_send, plane_recv):
    ys, zs, cores = sizes
    rows = tokens_ref.shape[0]
    count, _, capacity, width = out_ref.shape
    halves = 2
    half = rows // halves
    y, z, c = (lax.axis_index(a) for a in SEQ)
    right, left = lax.rem(z + 1, zs), lax.rem(z + zs - 1, zs)
    peers = []
    for p in range(1, count):
        peers.append({"seq_0": lax.rem(y + p // cores, ys), "seq_2": lax.rem(c + p % cores, cores)})

    barrier = pltpu.get_barrier_semaphore()
    for target in [{"seq_1": right}, {"seq_1": left}] + peers:
        pl.semaphore_signal(barrier, inc=1, device_id=target, device_id_type=MESH)

    place = lax.broadcasted_iota(jnp.int32, (count, rows), 0)
    experts = (
        lax.rem(y + place // cores, ys) * (zs * cores) + z * cores + lax.rem(c + lax.rem(place, cores), cores)
    )
    upper = (
        lax.broadcasted_iota(jnp.int32, (rows, rows), 0)
        < lax.broadcasted_iota(jnp.int32, (rows, rows), 1)
    ).astype(BF16)
    slot_of = lax.broadcasted_iota(jnp.int32, (capacity, rows), 0).astype(F32)

    def token_copy(source, slot, part, target):
        rng = pl.ds(part * half, half)
        return pltpu.make_async_remote_copy(
            src_ref=source.at[rng, :], dst_ref=held.at[slot, rng, :],
            send_sem=tok_send.at[slot, part], recv_sem=tok_recv.at[slot, part],
            device_id={"seq_1": target}, device_id_type=MESH)

    def ids_copy(source, slot, target):
        return pltpu.make_async_remote_copy(
            src_ref=source, dst_ref=ids.at[slot],
            send_sem=ids_send.at[slot], recv_sem=ids_recv.at[slot],
            device_id={"seq_1": target}, device_id_type=MESH)

    def plane_copy(slot, p):
        return pltpu.make_async_remote_copy(
            src_ref=stage.at[slot, p - 1], dst_ref=out_ref.at[p, slot],
            send_sem=plane_send.at[slot], recv_sem=plane_recv.at[slot],
            device_id=peers[p - 1], device_id_type=MESH)

    def choose(slot, tokens, names):
        named = jnp.zeros((count, rows), F32)
        for k in range(names.shape[0]):
            named += (names[k : k + 1, :] == experts).astype(F32)
        before = dot(named.astype(BF16), upper)
        where = jnp.where(named > 0.0, before, -1.0)
        picker = jnp.concatenate(
            [(where[p : p + 1, :] == slot_of).astype(BF16) for p in range(count)], axis=0
        )
        chosen = dot(picker, tokens).astype(BF16)
        out_ref[0, slot] = chosen[:capacity]
        for p in range(1, count):
            stage[slot, p - 1] = chosen[p * capacity : (p + 1) * capacity]
        for p in sorted(range(1, count), key=lambda p: abs(p // cores - ys // 2)):
            plane_copy(slot, p).start()

    pl.semaphore_wait(barrier, count + 1)
    ups = zs // 2
    ids_copy(routing_ref, 1, right).start()
    ids_copy(routing_ref, zs - 1, left).start()
    for part in range(halves):
        token_copy(tokens_ref, 1, part, right).start()
        token_copy(tokens_ref, zs - 1, part, left).start()

    def take(slot, part, onward, target):
        token_copy(held.at[slot], slot, part, target).wait_recv()
        if onward is not None:
            token_copy(held.at[slot], onward, part, target).start()

    def take_ids(slot, onward, target):
        ids_copy(ids.at[slot], slot, target).wait_recv()
        if onward is not None:
            ids_copy(ids.at[slot], onward, target).start()

    def lead(d):
        take_ids(d, d + 1, right)
        take(d, 0, d + 1, right)
        take_ids(zs - d, zs - d - 1, left)
        take(zs - d, 0, zs - d - 1, left)

    def follow(d):
        take(d, 1, d + 1, right)
        take(zs - d, 1, zs - d - 1, left)

    def arrived(slot):
        pltpu.make_async_remote_copy(
            src_ref=stage.at[slot], dst_ref=out_ref.at[pl.ds(1, count - 1), slot],
            send_sem=plane_send.at[slot], recv_sem=plane_recv.at[slot],
            device_id=peers[0], device_id_type=MESH).wait()
        return out_ref[:, slot].reshape(count * capacity, width)

    def accumulate(one, other):
        block = jnp.concatenate([arrived(one), arrived(other)], axis=0)
        gate = dot(block, gate_ref[...])
        upward = dot(block, up_ref[...])
        hidden = (gate / (1.0 + jnp.exp(-gate)) * upward).astype(BF16)
        for b, (i, j) in enumerate(BLOCKS):
            first = hidden[:, i * LANES : (i + 1) * LANES]
            second = hidden[:, j * LANES : (j + 1) * LANES]
            gram[:, b * LANES : (b + 1) * LANES] += dot(first, second, ((0,), (0,)))

    lead(1)
    choose(0, tokens_ref[...], routing_ref[...])
    gram[...] = jnp.zeros_like(gram)
    follow(1)

    def step(d, _):
        lead(d)
        choose(d - 1, held[d - 1], ids[d - 1])
        follow(d)
        choose(zs - d + 1, held[zs - d + 1], ids[zs - d + 1])

        @pl.when(d > 2)
        def _():
            accumulate(d - 2, zs - d + 2)

        return 0

    lax.fori_loop(2, ups - 1, step, 0)
    low, high = ups - 1, ups + 1
    take_ids(low, ups, right)
    take(low, 0, ups, right)
    take_ids(high, None, left)
    take(high, 0, None, left)
    choose(low - 1, held[low - 1], ids[low - 1])
    take(low, 1, None, right)
    take(high, 1, ups, left)
    choose(high + 1, held[high + 1], ids[high + 1])
    choose(low, held[low], ids[low])
    choose(high, held[high], ids[high])
    accumulate(low - 2, high + 2)
    take_ids(ups, None, right)
    take(ups, 0, None, right)
    take(ups, 1, None, left)
    choose(ups, held[ups], ids[ups])
    accumulate(low - 1, high + 1)
    accumulate(low, high)
    accumulate(0, ups)

    def sent(slot, _):
        for part in range(halves):
            token_copy(tokens_ref, slot, part, right).wait_send()
        ids_copy(routing_ref, slot, right).wait_send()
        return 0

    lax.fori_loop(1, zs, sent, 0)


def partner(i, sizes, here, sign):
    ys, zs, cores = sizes
    y, z, c = here
    dc = lax.rem(i, cores)
    rest = i // cores
    dy = lax.rem(rest, ys)
    zi = rest // ys
    dz = lax.rem(lax.rem(zi, 2) * ((zi + 1) // 2) + (1 - lax.rem(zi, 2)) * (zs - zi // 2), zs)
    if sign > 0:
        to = (lax.rem(y + dy, ys), lax.rem(z + dz, zs), lax.rem(c + dc, cores))
    else:
        to = (lax.rem(y + ys - dy, ys), lax.rem(z + zs - dz, zs), lax.rem(c + cores - dc, cores))
    return to, dict(zip(SEQ, to)), (to[0] * zs + to[1]) * cores + to[2]


def inverse(block, pivots=4):
    size = block.shape[0]
    lanes = lax.broadcasted_iota(jnp.int32, (8, size), 1)
    all_lanes = lax.broadcasted_iota(jnp.int32, (size, size), 1)
    subs = lax.broadcasted_iota(jnp.int32, (8, size), 0)

    def spread(x):
        return jnp.broadcast_to(x, (8, size))

    for k in range(0, size, pivots):
        own, row = 8 * (k // 8), k % 8
        rows = block[own : own + 8]
        mine = [spread(rows[:, k + j : k + j + 1]) for j in range(pivots)]
        inside = (lanes >= k) & (lanes < k + pivots)
        y = [
            jnp.where(
                lanes == k + j, 1.0, jnp.where(inside, 0.0, spread(rows[row + j : row + j + 1]))
            )
            for j in range(pivots)
        ]
        a = [[None] * pivots for _ in range(pivots)]
        for i in range(pivots):
            for j in range(i, pivots):
                a[i][j] = spread(mine[j][row + i : row + i + 1])
        d = [None] * pivots
        low = [[None] * pivots for _ in range(pivots)]
        for i in range(pivots):
            d[i] = 1.0 / a[i][i]
            for j in range(i + 1, pivots):
                low[j][i] = a[i][j] * d[i]
            for j in range(i + 1, pivots):
                for m in range(j, pivots):
                    a[j][m] = a[j][m] - low[j][i] * a[i][m]
                y[j] = y[j] - low[j][i] * y[i]
        y = [y[i] * d[i] for i in range(pivots)]
        for i in range(pivots - 1, -1, -1):
            for j in range(i):
                y[j] = y[j] - low[i][j] * y[i]
        fresh = jnp.where((all_lanes >= k) & (all_lanes < k + pivots), 0.0, block)
        for j in range(pivots):
            fresh = fresh - block[:, k + j : k + j + 1] * y[j][:1]
        fixed = fresh[own : own + 8]
        for j in range(pivots):
            fixed = jnp.where(subs == row + j, y[j], fixed)
        pieces = [fresh[:own], fixed, fresh[own + 8 :]]
        block = jnp.concatenate([p for p in pieces if p.shape[0]], axis=0)
    return block


def solve(a, right):
    nt, tn = ((1,), (1,)), ((0,), (0,))
    a00, a10, a11, a20, a21, a22 = a
    d0 = inverse(a00)
    l10 = dot(a10, d0, precision=HI)
    l20 = dot(a20, d0, precision=HI)
    a11 = a11 - dot(l10, a10, nt, precision=HI)
    d1 = inverse(a11)
    a21 = a21 - dot(l20, a10, nt, precision=HI)
    a22 = a22 - dot(l20, a20, nt, precision=HI)
    y1 = right[1] - dot(l10, right[0], precision=HI)
    z0 = dot(d0, right[0], precision=HI)
    l21 = dot(a21, d1, precision=HI)
    a22 = a22 - dot(l21, a21, nt, precision=HI)
    d2 = inverse(a22)
    y2 = right[2] - dot(l20, right[0], precision=HI) - dot(l21, y1, precision=HI)
    z1 = dot(d1, y1, precision=HI)
    x2 = dot(d2, y2, precision=HI)
    x1 = z1 - dot(l21, x2, tn, precision=HI)
    x0 = z0 - dot(l10, x1, tn, precision=HI) - dot(l20, x2, tn, precision=HI)
    return x0, x1, x2


def as_column(row, count, repeat=1):
    size = row.shape[1]
    shape = (count * repeat, size)
    hit = lax.broadcasted_iota(jnp.int32, shape, 0) // repeat == lax.broadcasted_iota(
        jnp.int32, shape, 1
    )
    return jnp.sum(jnp.where(hit, jnp.broadcast_to(row, shape), 0.0), axis=1, keepdims=True)


def tables(cluster_ref, owners_ref, ways):
    cluster = cluster_ref[...].astype(F32)
    owners = owners_ref[...].astype(F32)
    experts, clusters = cluster.shape[1], owners.shape[1]
    same = (as_column(cluster, experts) == cluster).astype(F32)

    owner = as_column(owners, clusters)
    square = (clusters, clusters)
    earlier = lax.broadcasted_iota(jnp.int32, square, 1) < lax.broadcasted_iota(jnp.int32, square, 0)
    ranking = jnp.sum(jnp.where((owner == owners) & earlier, 1.0, 0.0), axis=1, keepdims=True)
    slots = owner * OWN + ranking
    shape = (clusters, experts)
    member = lax.broadcasted_iota(jnp.int32, shape, 0).astype(F32) == cluster
    member_slot = jnp.sum(jnp.where(member, slots, 0.0), axis=0, keepdims=True)

    shape = (experts * ways, experts)
    row = lax.broadcasted_iota(jnp.int32, shape, 0)
    mine = as_column(cluster, experts, ways) == cluster
    held = member_slot == (row // ways).astype(F32)
    router = jnp.where(row % ways == 0, mine.astype(F32), held.astype(F32)).astype(BF16)
    return same, router


def merge_kernel(sizes, cuts, tokens_ref, routing_ref, gate_ref, up_ref, down_ref, cluster_ref,
                 owners_ref, b_in, gram, whole, g_out, g_in, s_out, s_in,
                 m_out, m_in, wide, mixed, b_out,
                 g_sems, s_sems, m_sems, b_sems, local_sem, *spread):
    n = sizes[0] * sizes[1] * sizes[2]
    here = tuple(lax.axis_index(x) for x in SEQ)
    me = (here[0] * sizes[1] + here[1]) * sizes[2] + here[2]
    blocks = len(BLOCKS)
    per = blocks // cuts
    size, width = down_ref.shape
    wide_groups = width // LANES
    parts = size // LANES
    tall = LANES // 8

    gather_gram(sizes, tokens_ref, routing_ref, gate_ref, up_ref, gram, *spread)
    eye = (
        lax.broadcasted_iota(jnp.int32, (LANES, LANES), 0)
        == lax.broadcasted_iota(jnp.int32, (LANES, LANES), 1)
    ).astype(F32)
    for b, (i, j) in enumerate(BLOCKS):
        if i == j:
            gram[:, b * LANES : (b + 1) * LANES] += ridge_weight * eye
        h, k = b // per, b % per
        g_out[h, pl.ds(k, n, stride=8), :] = gram[:, b * LANES : (b + 1) * LANES]

    def send(src, dst, sems, h):
        own = pltpu.make_async_copy(src(me), dst(me), local_sem)
        own.start()

        def one(i, _):
            _, to, index = partner(n - i, sizes, here, 1)
            pltpu.make_async_remote_copy(
                src_ref=src(index), dst_ref=dst(me), send_sem=sems.at[0, h], recv_sem=sems.at[1, h],
                device_id=to, device_id_type=MESH).start()
            return 0

        lax.fori_loop(1, n, one, 0)
        own.wait()

    def settle(ref, sems, h):
        pltpu.make_async_remote_copy(
            src_ref=ref, dst_ref=ref, send_sem=sems.at[0, h], recv_sem=sems.at[1, h],
            device_id={"seq_0": 0}, device_id_type=MESH).wait()

    def lines(ref, h):
        return lambda i: ref.at[h, pl.ds(pl.multiple_of(i * 8, 8), per), :]

    def settle_lines(ref, sems, h):
        settle(ref.at[h, pl.ds(0, (n - 1) * per), :], sems, h)

    for h in range(cuts):
        send(lines(g_out, h), lines(g_in, h), g_sems, h)

    ways = b_in.shape[2]
    same, router = tables(cluster_ref, owners_ref, ways)
    own = [gram[:, b * LANES : (b + 1) * LANES] for b in range(blocks)]
    whole[0] = jnp.concatenate([own[0], own[1].T, own[3].T], axis=1)
    whole[1] = jnp.concatenate([own[1], own[2], own[4].T], axis=1)
    whole[2] = jnp.concatenate([own[3], own[4], own[5]], axis=1)
    for h in range(cuts):
        settle_lines(g_in, g_sems, h)
        for k in range(per):
            s_out[h, pl.ds(k, n, stride=8), :] = dot(
                same, g_in[h, pl.ds(k, n, stride=8), :], precision=HI)
        send(lines(s_out, h), lines(s_in, h), s_sems, h)
    for h in range(cuts):
        settle_lines(s_in, s_sems, h)

    solved = solve(
        [s_in[b // per, pl.ds(b % per, n, stride=8), :] for b in range(blocks)],
        [whole[i] for i in range(parts)])
    down = down_ref[...]
    for p in range(parts):
        high = solved[p].astype(BF16)
        low = (solved[p] - high.astype(F32)).astype(BF16)
        part = dot(high, down) + dot(low, down)
        for g in range(tall):
            for c in range(wide_groups):
                m_out[p, g * wide_groups + c] = part[
                    g * 8 : g * 8 + 8, c * LANES : (c + 1) * LANES].astype(BF16)
        send(lambda i: m_out.at[p, i], lambda i: m_in.at[p, i], m_sems, p)

    for p in range(parts):
        settle(m_in.at[p, pl.ds(0, n - 1)], m_sems, p)

        def widen(i, _):
            wide[pl.ds(pl.multiple_of(i * 8, 8), 8), :] = m_in[p, i].astype(F32)
            return 0

        lax.fori_loop(0, n, widen, 0, unroll=8)

        def mix(r, _):
            x = wide[pl.ds(r, n, stride=8), :].astype(BF16)
            mixed[pl.ds(r, ways * n, stride=8), :] = dot(router, x)
            return 0

        lax.fori_loop(0, 8, mix, 0, unroll=4)

        def narrow(i, _):
            for w in range(ways):
                b_out[p, i, w] = mixed[pl.ds(pl.multiple_of((i * ways + w) * 8, 8), 8), :].astype(BF16)
            return 0

        lax.fori_loop(0, n, narrow, 0, unroll=4)
        send(lambda i: b_out.at[p, i], lambda i: b_in.at[p, i], b_sems, p)

    for p in range(parts):
        settle(b_in.at[p, pl.ds(0, n - 1)], b_sems, p)


def merge(tokens, routing_t, gate, up, down, cluster_of, owners, sizes, capacity, cuts=2, ways=2):
    ys, zs, cores = sizes
    n = ys * zs * cores
    count = ys * cores
    rows, features = tokens.shape
    size, width = down.shape
    parts = size // LANES
    blocks = len(BLOCKS)
    vm = pl.BlockSpec(memory_space=pltpu.VMEM)
    lines = pltpu.VMEM((cuts, n * 8, LANES), F32)
    dma = pltpu.SemaphoreType.DMA
    return pl.pallas_call(
        functools.partial(merge_kernel, sizes, cuts),
        out_shape=jax.ShapeDtypeStruct((parts, n, ways, 8, LANES), BF16),
        in_specs=[vm] * 7,
        out_specs=vm,
        scratch_shapes=[
            pltpu.VMEM((LANES, blocks * LANES), F32),
            pltpu.VMEM((parts, LANES, size), F32),
            lines, lines, lines, lines,
            pltpu.VMEM((parts, n, 8, LANES), BF16),
            pltpu.VMEM((parts, n, 8, LANES), BF16),
            pltpu.VMEM((n * 8, LANES), F32),
            pltpu.VMEM((ways * n * 8, LANES), F32),
            pltpu.VMEM((parts, n, ways, 8, LANES), BF16),
            dma((2, cuts)), dma((2, cuts)), dma((2, parts)), dma((2, parts)), dma,
            pltpu.VMEM((count, zs, capacity, features), BF16),
            pltpu.VMEM((zs, rows, features), BF16),
            pltpu.VMEM((zs,) + routing_t.shape, jnp.int32),
            pltpu.VMEM((zs, count - 1, capacity, features), BF16),
            dma((zs, 2)), dma((zs, 2)), dma((zs,)), dma((zs,)), dma((zs,)), dma((zs,)),
        ],
        compiler_params=pltpu.CompilerParams(collective_id=0, has_side_effects=True),
    )(tokens, routing_t, gate, up, down, cluster_of.reshape(1, -1), owners.reshape(1, -1))


def finish_kernel(chunks_ref, down_ref, diff_ref, slot_ref):
    wide_groups = down_ref.shape[1] // LANES
    for g in range(down_ref.shape[0] // 16):
        rows = slice(g * 16, g * 16 + 16)
        for c in range(wide_groups):
            columns = slice(c * LANES, (c + 1) * LANES)
            upper = g * 2 * wide_groups + c
            mine, held = (
                jnp.concatenate(
                    [chunks_ref[0, upper, w], chunks_ref[0, upper + wide_groups, w]], axis=0)
                for w in range(2)
            )
            diff_ref[rows, columns] = (
                mine.astype(F32) - down_ref[rows, columns].astype(F32)
            ).astype(BF16)
            slot_ref[rows, columns] = held


def finish(chunks, down):
    size, width = down.shape
    block = pl.BlockSpec((LANES, width), lambda p: (p, 0))
    return pl.pallas_call(
        finish_kernel,
        out_shape=(jax.ShapeDtypeStruct((size, width), BF16),) * 2,
        grid=(chunks.shape[0],),
        in_specs=[pl.BlockSpec((1,) + chunks.shape[1:], lambda p: (p, 0, 0, 0, 0)), block],
        out_specs=(block, block),
    )(chunks, down)


def body(tokens, routing, gate_weight, up_weight, down_weight, cluster_of, owners):
    ys, zs, cores = (lax.axis_size(a) for a in SEQ)
    rows_dev = tokens.shape[0]
    topk = routing.shape[1]
    experts = cluster_of.shape[0]
    capacity = min(rows_dev, max(2, 2 * rows_dev * topk // experts))

    chunks = merge(
        tokens, routing.T, gate_weight[0], up_weight[0], down_weight[0], cluster_of, owners,
        (ys, zs, cores), capacity)
    differences, merged_slots = finish(chunks, down_weight[0])
    return (differences[None], merged_slots[None])


def solution(mesh):
    finer = Mesh(
        mesh.devices.reshape(4, 16, 2, mesh.shape["layer"]), ("seq_0", "seq_1", "seq_2", "layer")
    )
    return jax.shard_map(
        body,
        mesh=finer,
        in_specs=(
            P(LAYER_SEQ, None),
            P(LAYER_SEQ, None),
            P(LAYER_SEQ, None, None),
            P(LAYER_SEQ, None, None),
            P(LAYER_SEQ, None, None),
            P("layer"),
            P("layer"),
        ),
        out_specs=(P(LAYER_SEQ, None, None), P(LAYER_SEQ, None, None)),
        check_vma=False,
    )
```

```python
import functools

import jax
import jax.numpy as jnp
from jax import lax
from jax.experimental import pallas as pl
from jax.experimental.pallas import tpu as pltpu
from jax.sharding import Mesh
from jax.sharding import PartitionSpec as P

OWN = 1
SEQ = ("seq_0", "seq_1", "seq_2")
PLANE = ("seq_0", "seq_2")
LAYER_SEQ = ("layer", "seq_0", "seq_1", "seq_2")
HI = lax.Precision.HIGHEST
F32 = jnp.float32
BF16 = jnp.bfloat16
MESH = pl.DeviceIdType.MESH

ridge_weight = 32.0
LANES = 128
BLOCKS = ((0, 0), (1, 0), (1, 1), (2, 0), (2, 1), (2, 2))


def dot(a, b, dims=((1,), (0,)), precision=None):
    return lax.dot_general(a, b, (dims, ((), ())), preferred_element_type=F32, precision=precision)


def gather_gram(sizes, tokens_ref, routing_ref, gate_ref, up_ref, gram, out_ref, held, ids, stage,
                tok_send, tok_recv, ids_send, ids_recv, plane_send, plane_recv):
    ys, zs, cores = sizes
    rows = tokens_ref.shape[0]
    count, _, capacity, width = out_ref.shape
    halves = 2
    half = rows // halves
    y, z, c = (lax.axis_index(a) for a in SEQ)
    right, left = lax.rem(z + 1, zs), lax.rem(z + zs - 1, zs)
    peers = []
    for p in range(1, count):
        peers.append({"seq_0": lax.rem(y + p // cores, ys), "seq_2": lax.rem(c + p % cores, cores)})

    barrier = pltpu.get_barrier_semaphore()
    for target in [{"seq_1": right}, {"seq_1": left}] + peers:
        pl.semaphore_signal(barrier, inc=1, device_id=target, device_id_type=MESH)

    place = lax.broadcasted_iota(jnp.int32, (count, rows), 0)
    experts = (
        lax.rem(y + place // cores, ys) * (zs * cores) + z * cores + lax.rem(c + lax.rem(place, cores), cores)
    )
    upper = (
        lax.broadcasted_iota(jnp.int32, (rows, rows), 0)
        < lax.broadcasted_iota(jnp.int32, (rows, rows), 1)
    ).astype(BF16)
    slot_of = lax.broadcasted_iota(jnp.int32, (capacity, rows), 0).astype(F32)

    def token_copy(source, slot, part, target):
        rng = pl.ds(part * half, half)
        return pltpu.make_async_remote_copy(
            src_ref=source.at[rng, :], dst_ref=held.at[slot, rng, :],
            send_sem=tok_send.at[slot, part], recv_sem=tok_recv.at[slot, part],
            device_id={"seq_1": target}, device_id_type=MESH)

    def ids_copy(source, slot, target):
        return pltpu.make_async_remote_copy(
            src_ref=source, dst_ref=ids.at[slot],
            send_sem=ids_send.at[slot], recv_sem=ids_recv.at[slot],
            device_id={"seq_1": target}, device_id_type=MESH)

    def plane_copy(slot, p):
        return pltpu.make_async_remote_copy(
            src_ref=stage.at[slot, p - 1], dst_ref=out_ref.at[p, slot],
            send_sem=plane_send.at[slot], recv_sem=plane_recv.at[slot],
            device_id=peers[p - 1], device_id_type=MESH)

    def choose(slot, tokens, names):
        named = jnp.zeros((count, rows), F32)
        for k in range(names.shape[0]):
            named += (names[k : k + 1, :] == experts).astype(F32)
        before = dot(named.astype(BF16), upper)
        where = jnp.where(named > 0.0, before, -1.0)
        picker = jnp.concatenate(
            [(where[p : p + 1, :] == slot_of).astype(BF16) for p in range(count)], axis=0
        )
        chosen = dot(picker, tokens).astype(BF16)
        out_ref[0, slot] = chosen[:capacity]
        for p in range(1, count):
            stage[slot, p - 1] = chosen[p * capacity : (p + 1) * capacity]
        for p in sorted(range(1, count), key=lambda p: abs(p // cores - ys // 2)):
            plane_copy(slot, p).start()

    pl.semaphore_wait(barrier, count + 1)
    ups = zs // 2
    ids_copy(routing_ref, 1, right).start()
    ids_copy(routing_ref, zs - 1, left).start()
    for part in range(halves):
        token_copy(tokens_ref, 1, part, right).start()
        token_copy(tokens_ref, zs - 1, part, left).start()

    def take(slot, part, onward, target):
        token_copy(held.at[slot], slot, part, target).wait_recv()
        if onward is not None:
            token_copy(held.at[slot], onward, part, target).start()

    def take_ids(slot, onward, target):
        ids_copy(ids.at[slot], slot, target).wait_recv()
        if onward is not None:
            ids_copy(ids.at[slot], onward, target).start()

    def lead(d):
        take_ids(d, d + 1, right)
        take(d, 0, d + 1, right)
        take_ids(zs - d, zs - d - 1, left)
        take(zs - d, 0, zs - d - 1, left)

    def follow(d):
        take(d, 1, d + 1, right)
        take(zs - d, 1, zs - d - 1, left)

    def arrived(slot):
        pltpu.make_async_remote_copy(
            src_ref=stage.at[slot], dst_ref=out_ref.at[pl.ds(1, count - 1), slot],
            send_sem=plane_send.at[slot], recv_sem=plane_recv.at[slot],
            device_id=peers[0], device_id_type=MESH).wait()
        return out_ref[:, slot].reshape(count * capacity, width)

    def accumulate(one, other):
        block = jnp.concatenate([arrived(one), arrived(other)], axis=0)
        gate = dot(block, gate_ref[...])
        upward = dot(block, up_ref[...])
        hidden = (gate / (1.0 + jnp.exp(-gate)) * upward).astype(BF16)
        for b, (i, j) in enumerate(BLOCKS):
            first = hidden[:, i * LANES : (i + 1) * LANES]
            second = hidden[:, j * LANES : (j + 1) * LANES]
            gram[:, b * LANES : (b + 1) * LANES] += dot(first, second, ((0,), (0,)))

    lead(1)
    choose(0, tokens_ref[...], routing_ref[...])
    gram[...] = jnp.zeros_like(gram)
    follow(1)

    def step(d, _):
        lead(d)
        choose(d - 1, held[d - 1], ids[d - 1])
        follow(d)
        choose(zs - d + 1, held[zs - d + 1], ids[zs - d + 1])

        @pl.when(d > 2)
        def _():
            accumulate(d - 2, zs - d + 2)

        return 0

    lax.fori_loop(2, ups - 1, step, 0)
    low, high = ups - 1, ups + 1
    take_ids(low, ups, right)
    take(low, 0, ups, right)
    take_ids(high, None, left)
    take(high, 0, None, left)
    choose(low - 1, held[low - 1], ids[low - 1])
    take(low, 1, None, right)
    take(high, 1, ups, left)
    choose(high + 1, held[high + 1], ids[high + 1])
    choose(low, held[low], ids[low])
    choose(high, held[high], ids[high])
    accumulate(low - 2, high + 2)
    take_ids(ups, None, right)
    take(ups, 0, None, right)
    take(ups, 1, None, left)
    choose(ups, held[ups], ids[ups])
    accumulate(low - 1, high + 1)
    accumulate(low, high)
    accumulate(0, ups)

    def sent(slot, _):
        for part in range(halves):
            token_copy(tokens_ref, slot, part, right).wait_send()
        ids_copy(routing_ref, slot, right).wait_send()
        return 0

    lax.fori_loop(1, zs, sent, 0)


def partner(i, sizes, here, sign):
    ys, zs, cores = sizes
    y, z, c = here
    dc = lax.rem(i, cores)
    rest = i // cores
    dy = lax.rem(rest, ys)
    zi = rest // ys
    dz = lax.rem(lax.rem(zi, 2) * ((zi + 1) // 2) + (1 - lax.rem(zi, 2)) * (zs - zi // 2), zs)
    if sign > 0:
        to = (lax.rem(y + dy, ys), lax.rem(z + dz, zs), lax.rem(c + dc, cores))
    else:
        to = (lax.rem(y + ys - dy, ys), lax.rem(z + zs - dz, zs), lax.rem(c + cores - dc, cores))
    return to, dict(zip(SEQ, to)), (to[0] * zs + to[1]) * cores + to[2]


def inverse(block, pivots=8):
    size = block.shape[0]
    lanes = lax.broadcasted_iota(jnp.int32, (8, size), 1)
    all_lanes = lax.broadcasted_iota(jnp.int32, (size, size), 1)
    subs = lax.broadcasted_iota(jnp.int32, (8, size), 0)

    def spread(x):
        return jnp.broadcast_to(x, (8, size))

    for k in range(0, size, pivots):
        own, row = 8 * (k // 8), k % 8
        rows = block[own : own + 8]
        mine = [spread(rows[:, k + j : k + j + 1]) for j in range(pivots)]
        inside = (lanes >= k) & (lanes < k + pivots)
        y = [
            jnp.where(
                lanes == k + j, 1.0, jnp.where(inside, 0.0, spread(rows[row + j : row + j + 1]))
            )
            for j in range(pivots)
        ]
        a = [[None] * pivots for _ in range(pivots)]
        for i in range(pivots):
            for j in range(i, pivots):
                a[i][j] = spread(mine[j][row + i : row + i + 1])
        d = [None] * pivots
        low = [[None] * pivots for _ in range(pivots)]
        for i in range(pivots):
            d[i] = 1.0 / a[i][i]
            for j in range(i + 1, pivots):
                low[j][i] = a[i][j] * d[i]
            for j in range(i + 1, pivots):
                for m in range(j, pivots):
                    a[j][m] = a[j][m] - low[j][i] * a[i][m]
                y[j] = y[j] - low[j][i] * y[i]
        y = [y[i] * d[i] for i in range(pivots)]
        for i in range(pivots - 1, -1, -1):
            for j in range(i):
                y[j] = y[j] - low[i][j] * y[i]
        fresh = jnp.where((all_lanes >= k) & (all_lanes < k + pivots), 0.0, block)
        for j in range(pivots):
            fresh = fresh - block[:, k + j : k + j + 1] * y[j][:1]
        fixed = fresh[own : own + 8]
        for j in range(pivots):
            fixed = jnp.where(subs == row + j, y[j], fixed)
        pieces = [fresh[:own], fixed, fresh[own + 8 :]]
        block = jnp.concatenate([p for p in pieces if p.shape[0]], axis=0)
    return block


def square(which):
    return lax.broadcasted_iota(jnp.int32, (LANES, LANES), which)


def fold(blocks):
    a00, a10, a11, a20, a21, a22 = blocks
    row, col = square(0), square(1)
    diagonal = jnp.sum(jnp.where(row == col, a11, 0.0), axis=0, keepdims=True)
    spare = jnp.where(row == 0, diagonal, 0.0)
    spare = jnp.where((row == 1) & (col == 2), diagonal[:, :1], spare)
    return (a10, a20, jnp.where(row >= col, a00, a11)), (a21, jnp.where(row >= col, a22, spare))


def lower_of(x):
    row, col = square(0), square(1)
    return jnp.where(row >= col, x, 0.0) + jnp.where(row > col, x, 0.0).T


def solve(first, rest, right):
    nt, tn = ((1,), (1,)), ((0,), (0,))
    row, col = square(0), square(1)
    a10, a20, mixed = first()
    d0 = inverse(lower_of(mixed))
    l10 = dot(a10, d0, precision=HI)
    l20 = dot(a20, d0, precision=HI)
    y1 = right[1] - dot(l10, right[0], precision=HI)
    z0 = dot(d0, right[0], precision=HI)
    down11 = dot(l10, a10, nt, precision=HI)
    down21 = dot(l20, a10, nt, precision=HI)
    down22 = dot(l20, a20, nt, precision=HI)
    above = jnp.where(row < col, mixed, 0.0)
    above = above + above.T
    a21, last = rest()
    diagonal = jnp.where(col[:1] == 0, last[1:2, 2:3], last[:1])
    a11 = above + jnp.where(row == col, diagonal, 0.0) - down11
    d1 = inverse(a11)
    a21 = a21 - down21
    a22 = lower_of(last) - down22
    l21 = dot(a21, d1, precision=HI)
    a22 = a22 - dot(l21, a21, nt, precision=HI)
    d2 = inverse(a22)
    y2 = right[2] - dot(l20, right[0], precision=HI) - dot(l21, y1, precision=HI)
    z1 = dot(d1, y1, precision=HI)
    x2 = dot(d2, y2, precision=HI)
    x1 = z1 - dot(l21, x2, tn, precision=HI)
    x0 = z0 - dot(l10, x1, tn, precision=HI) - dot(l20, x2, tn, precision=HI)
    return x0, x1, x2


def as_column(row, count, repeat=1):
    size = row.shape[1]
    shape = (count * repeat, size)
    hit = lax.broadcasted_iota(jnp.int32, shape, 0) // repeat == lax.broadcasted_iota(
        jnp.int32, shape, 1
    )
    return jnp.sum(jnp.where(hit, jnp.broadcast_to(row, shape), 0.0), axis=1, keepdims=True)


def tables(cluster_ref, owners_ref, ways):
    cluster = cluster_ref[...].astype(F32)
    owners = owners_ref[...].astype(F32)
    experts, clusters = cluster.shape[1], owners.shape[1]
    same = (as_column(cluster, experts) == cluster).astype(F32)

    owner = as_column(owners, clusters)
    square = (clusters, clusters)
    earlier = lax.broadcasted_iota(jnp.int32, square, 1) < lax.broadcasted_iota(jnp.int32, square, 0)
    ranking = jnp.sum(jnp.where((owner == owners) & earlier, 1.0, 0.0), axis=1, keepdims=True)
    slots = owner * OWN + ranking
    shape = (clusters, experts)
    member = lax.broadcasted_iota(jnp.int32, shape, 0).astype(F32) == cluster
    member_slot = jnp.sum(jnp.where(member, slots, 0.0), axis=0, keepdims=True)

    shape = (experts * ways, experts)
    row = lax.broadcasted_iota(jnp.int32, shape, 0)
    mine = as_column(cluster, experts, ways) == cluster
    held = member_slot == (row // ways).astype(F32)
    router = jnp.where(row % ways == 0, mine.astype(F32), held.astype(F32)).astype(BF16)
    return same, router


def merge_kernel(sizes, tokens_ref, routing_ref, gate_ref, up_ref, down_ref, cluster_ref,
                 owners_ref, b_in, gram, whole, g_out, g_in, s_out, s_in,
                 m_out, m_in, wide, mixed, b_out,
                 g_sems, s_sems, m_sems, b_sems, local_sem, *spread):
    n = sizes[0] * sizes[1] * sizes[2]
    here = tuple(lax.axis_index(x) for x in SEQ)
    me = (here[0] * sizes[1] + here[1]) * sizes[2] + here[2]
    blocks = len(BLOCKS)
    per = (3, 2)
    cuts = len(per)
    size, width = down_ref.shape
    wide_groups = width // LANES
    parts = size // LANES
    tall = LANES // 8

    gather_gram(sizes, tokens_ref, routing_ref, gate_ref, up_ref, gram, *spread)
    eye = (
        lax.broadcasted_iota(jnp.int32, (LANES, LANES), 0)
        == lax.broadcasted_iota(jnp.int32, (LANES, LANES), 1)
    ).astype(F32)
    for b, (i, j) in enumerate(BLOCKS):
        if i == j:
            gram[:, b * LANES : (b + 1) * LANES] += ridge_weight * eye
    own = [gram[:, b * LANES : (b + 1) * LANES] for b in range(blocks)]
    for h, squares in enumerate(fold(own)):
        for k in range(per[h]):
            g_out[h, pl.ds(k, n, stride=8), :] = squares[k]

    def send(src, dst, sems, h):
        own = pltpu.make_async_copy(src(me), dst(me), local_sem)
        own.start()

        def one(i, _):
            _, to, index = partner(n - i, sizes, here, 1)
            pltpu.make_async_remote_copy(
                src_ref=src(index), dst_ref=dst(me), send_sem=sems.at[0, h], recv_sem=sems.at[1, h],
                device_id=to, device_id_type=MESH).start()
            return 0

        lax.fori_loop(1, n, one, 0)
        own.wait()

    def settle(ref, sems, h):
        pltpu.make_async_remote_copy(
            src_ref=ref, dst_ref=ref, send_sem=sems.at[0, h], recv_sem=sems.at[1, h],
            device_id={"seq_0": 0}, device_id_type=MESH).wait()

    def lines(ref, h):
        return lambda i: ref.at[h, pl.ds(pl.multiple_of(i * 8, 8), per[h]), :]

    def settle_lines(ref, sems, h):
        settle(ref.at[h, pl.ds(0, (n - 1) * per[h]), :], sems, h)

    for h in range(cuts):
        send(lines(g_out, h), lines(g_in, h), g_sems, h)

    ways = b_in.shape[2]
    same, router = tables(cluster_ref, owners_ref, ways)
    whole[0] = jnp.concatenate([own[0], own[1].T, own[3].T], axis=1)
    whole[1] = jnp.concatenate([own[1], own[2], own[4].T], axis=1)
    whole[2] = jnp.concatenate([own[3], own[4], own[5]], axis=1)
    for h in range(cuts):
        settle_lines(g_in, g_sems, h)
        for k in range(per[h]):
            s_out[h, pl.ds(k, n, stride=8), :] = dot(
                same, g_in[h, pl.ds(k, n, stride=8), :], precision=HI)
        send(lines(s_out, h), lines(s_in, h), s_sems, h)

    def summed(h):
        settle_lines(s_in, s_sems, h)
        return [s_in[h, pl.ds(k, n, stride=8), :] for k in range(per[h])]

    solved = solve(lambda: summed(0), lambda: summed(1), [whole[i] for i in range(parts)])
    down = down_ref[...]
    for p in range(parts):
        high = solved[p].astype(BF16)
        low = (solved[p] - high.astype(F32)).astype(BF16)
        part = dot(high, down) + dot(low, down)
        for g in range(tall):
            for c in range(wide_groups):
                m_out[p, g * wide_groups + c] = part[
                    g * 8 : g * 8 + 8, c * LANES : (c + 1) * LANES].astype(BF16)
        send(lambda i: m_out.at[p, i], lambda i: m_in.at[p, i], m_sems, p)

    for p in range(parts):
        settle(m_in.at[p, pl.ds(0, n - 1)], m_sems, p)

        def widen(i, _):
            wide[pl.ds(pl.multiple_of(i * 8, 8), 8), :] = m_in[p, i].astype(F32)
            return 0

        lax.fori_loop(0, n, widen, 0, unroll=8)

        def mix(r, _):
            x = wide[pl.ds(r, n, stride=8), :].astype(BF16)
            mixed[pl.ds(r, ways * n, stride=8), :] = dot(router, x)
            return 0

        lax.fori_loop(0, 8, mix, 0, unroll=4)

        def narrow(i, _):
            for w in range(ways):
                b_out[p, i, w] = mixed[pl.ds(pl.multiple_of((i * ways + w) * 8, 8), 8), :].astype(BF16)
            return 0

        lax.fori_loop(0, n, narrow, 0, unroll=4)
        send(lambda i: b_out.at[p, i], lambda i: b_in.at[p, i], b_sems, p)

    for p in range(parts):
        settle(b_in.at[p, pl.ds(0, n - 1)], b_sems, p)


def merge(tokens, routing_t, gate, up, down, cluster_of, owners, sizes, capacity, cuts=2, ways=2):
    ys, zs, cores = sizes
    n = ys * zs * cores
    count = ys * cores
    rows, features = tokens.shape
    size, width = down.shape
    parts = size // LANES
    blocks = len(BLOCKS)
    vm = pl.BlockSpec(memory_space=pltpu.VMEM)
    lines = pltpu.VMEM((cuts, n * 8, LANES), F32)
    dma = pltpu.SemaphoreType.DMA
    return pl.pallas_call(
        functools.partial(merge_kernel, sizes),
        out_shape=jax.ShapeDtypeStruct((parts, n, ways, 8, LANES), BF16),
        in_specs=[vm] * 7,
        out_specs=vm,
        scratch_shapes=[
            pltpu.VMEM((LANES, blocks * LANES), F32),
            pltpu.VMEM((parts, LANES, size), F32),
            lines, lines, lines, lines,
            pltpu.VMEM((parts, n, 8, LANES), BF16),
            pltpu.VMEM((parts, n, 8, LANES), BF16),
            pltpu.VMEM((n * 8, LANES), F32),
            pltpu.VMEM((ways * n * 8, LANES), F32),
            pltpu.VMEM((parts, n, ways, 8, LANES), BF16),
            dma((2, cuts)), dma((2, cuts)), dma((2, parts)), dma((2, parts)), dma,
            pltpu.VMEM((count, zs, capacity, features), BF16),
            pltpu.VMEM((zs, rows, features), BF16),
            pltpu.VMEM((zs,) + routing_t.shape, jnp.int32),
            pltpu.VMEM((zs, count - 1, capacity, features), BF16),
            dma((zs, 2)), dma((zs, 2)), dma((zs,)), dma((zs,)), dma((zs,)), dma((zs,)),
        ],
        compiler_params=pltpu.CompilerParams(collective_id=0, has_side_effects=True),
    )(tokens, routing_t, gate, up, down, cluster_of.reshape(1, -1), owners.reshape(1, -1))


def finish_kernel(chunks_ref, down_ref, diff_ref, slot_ref):
    wide_groups = down_ref.shape[1] // LANES
    for g in range(down_ref.shape[0] // 16):
        rows = slice(g * 16, g * 16 + 16)
        for c in range(wide_groups):
            columns = slice(c * LANES, (c + 1) * LANES)
            upper = g * 2 * wide_groups + c
            mine, held = (
                jnp.concatenate(
                    [chunks_ref[0, upper, w], chunks_ref[0, upper + wide_groups, w]], axis=0)
                for w in range(2)
            )
            diff_ref[rows, columns] = (
                mine.astype(F32) - down_ref[rows, columns].astype(F32)
            ).astype(BF16)
            slot_ref[rows, columns] = held


def finish(chunks, down):
    size, width = down.shape
    block = pl.BlockSpec((LANES, width), lambda p: (p, 0))
    return pl.pallas_call(
        finish_kernel,
        out_shape=(jax.ShapeDtypeStruct((size, width), BF16),) * 2,
        grid=(chunks.shape[0],),
        in_specs=[pl.BlockSpec((1,) + chunks.shape[1:], lambda p: (p, 0, 0, 0, 0)), block],
        out_specs=(block, block),
    )(chunks, down)


def body(tokens, routing, gate_weight, up_weight, down_weight, cluster_of, owners):
    ys, zs, cores = (lax.axis_size(a) for a in SEQ)
    rows_dev = tokens.shape[0]
    topk = routing.shape[1]
    experts = cluster_of.shape[0]
    capacity = min(rows_dev, max(2, 2 * rows_dev * topk // experts))

    chunks = merge(
        tokens, routing.T, gate_weight[0], up_weight[0], down_weight[0], cluster_of, owners,
        (ys, zs, cores), capacity)
    differences, merged_slots = finish(chunks, down_weight[0])
    return (differences[None], merged_slots[None])


def solution(mesh):
    finer = Mesh(
        mesh.devices.reshape(4, 16, 2, mesh.shape["layer"]), ("seq_0", "seq_1", "seq_2", "layer")
    )
    return jax.shard_map(
        body,
        mesh=finer,
        in_specs=(
            P(LAYER_SEQ, None),
            P(LAYER_SEQ, None),
            P(LAYER_SEQ, None, None),
            P(LAYER_SEQ, None, None),
            P(LAYER_SEQ, None, None),
            P("layer"),
            P("layer"),
        ),
        out_specs=(P(LAYER_SEQ, None, None), P(LAYER_SEQ, None, None)),
        check_vma=False,
    )
```

```python
import functools

import jax
import jax.numpy as jnp
from jax import lax
from jax.experimental import pallas as pl
from jax.experimental.pallas import tpu as pltpu
from jax.sharding import Mesh
from jax.sharding import PartitionSpec as P

OWN = 1
SEQ = ("seq_0", "seq_1", "seq_2")
PLANE = ("seq_0", "seq_2")
LAYER_SEQ = ("layer", "seq_0", "seq_1", "seq_2")
HI = lax.Precision.HIGHEST
F32 = jnp.float32
BF16 = jnp.bfloat16
MESH = pl.DeviceIdType.MESH

ridge_weight = 32.0
LANES = 128
BLOCKS = ((0, 0), (1, 0), (1, 1), (2, 0), (2, 1), (2, 2))


def dot(a, b, dims=((1,), (0,)), precision=None):
    return lax.dot_general(a, b, (dims, ((), ())), preferred_element_type=F32, precision=precision)


def gather_gram(sizes, tokens_ref, routing_ref, gate_ref, up_ref, gram, out_ref, held, ids, stage,
                tok_send, tok_recv, ids_send, ids_recv, plane_send, plane_recv):
    ys, zs, cores = sizes
    rows = tokens_ref.shape[0]
    count, _, capacity, width = out_ref.shape
    halves = 2
    half = rows // halves
    y, z, c = (lax.axis_index(a) for a in SEQ)
    right, left = lax.rem(z + 1, zs), lax.rem(z + zs - 1, zs)
    peers = []
    for p in range(1, count):
        peers.append({"seq_0": lax.rem(y + p // cores, ys), "seq_2": lax.rem(c + p % cores, cores)})

    barrier = pltpu.get_barrier_semaphore()
    for target in [{"seq_1": right}, {"seq_1": left}] + peers:
        pl.semaphore_signal(barrier, inc=1, device_id=target, device_id_type=MESH)

    place = lax.broadcasted_iota(jnp.int32, (count, rows), 0)
    experts = (
        lax.rem(y + place // cores, ys) * (zs * cores) + z * cores + lax.rem(c + lax.rem(place, cores), cores)
    )
    upper = (
        lax.broadcasted_iota(jnp.int32, (rows, rows), 0)
        < lax.broadcasted_iota(jnp.int32, (rows, rows), 1)
    ).astype(BF16)
    slot_of = lax.broadcasted_iota(jnp.int32, (capacity, rows), 0).astype(F32)

    def token_copy(source, slot, part, target):
        rng = pl.ds(part * half, half)
        return pltpu.make_async_remote_copy(
            src_ref=source.at[rng, :], dst_ref=held.at[slot, rng, :],
            send_sem=tok_send.at[slot, part], recv_sem=tok_recv.at[slot, part],
            device_id={"seq_1": target}, device_id_type=MESH)

    def ids_copy(source, slot, target):
        return pltpu.make_async_remote_copy(
            src_ref=source, dst_ref=ids.at[slot],
            send_sem=ids_send.at[slot], recv_sem=ids_recv.at[slot],
            device_id={"seq_1": target}, device_id_type=MESH)

    def plane_copy(slot, p):
        return pltpu.make_async_remote_copy(
            src_ref=stage.at[slot, p - 1], dst_ref=out_ref.at[p, slot],
            send_sem=plane_send.at[slot], recv_sem=plane_recv.at[slot],
            device_id=peers[p - 1], device_id_type=MESH)

    def choose(slot, tokens, names):
        named = jnp.zeros((count, rows), F32)
        for k in range(names.shape[0]):
            named += (names[k : k + 1, :] == experts).astype(F32)
        before = dot(named.astype(BF16), upper)
        where = jnp.where(named > 0.0, before, -1.0)
        picker = jnp.concatenate(
            [(where[p : p + 1, :] == slot_of).astype(BF16) for p in range(count)], axis=0
        )
        chosen = dot(picker, tokens).astype(BF16)
        out_ref[0, slot] = chosen[:capacity]
        for p in range(1, count):
            stage[slot, p - 1] = chosen[p * capacity : (p + 1) * capacity]
        for p in sorted(range(1, count), key=lambda p: abs(p // cores - ys // 2)):
            plane_copy(slot, p).start()

    pl.semaphore_wait(barrier, count + 1)
    ups = zs // 2
    ids_copy(routing_ref, 1, right).start()
    ids_copy(routing_ref, zs - 1, left).start()
    for part in range(halves):
        token_copy(tokens_ref, 1, part, right).start()
        token_copy(tokens_ref, zs - 1, part, left).start()

    def take(slot, part, onward, target):
        token_copy(held.at[slot], slot, part, target).wait_recv()
        if onward is not None:
            token_copy(held.at[slot], onward, part, target).start()

    def take_ids(slot, onward, target):
        ids_copy(ids.at[slot], slot, target).wait_recv()
        if onward is not None:
            ids_copy(ids.at[slot], onward, target).start()

    def lead(d):
        take_ids(d, d + 1, right)
        take(d, 0, d + 1, right)
        take_ids(zs - d, zs - d - 1, left)
        take(zs - d, 0, zs - d - 1, left)

    def follow(d):
        take(d, 1, d + 1, right)
        take(zs - d, 1, zs - d - 1, left)

    def arrived(slot):
        pltpu.make_async_remote_copy(
            src_ref=stage.at[slot], dst_ref=out_ref.at[pl.ds(1, count - 1), slot],
            send_sem=plane_send.at[slot], recv_sem=plane_recv.at[slot],
            device_id=peers[0], device_id_type=MESH).wait()
        return out_ref[:, slot].reshape(count * capacity, width)

    def accumulate(one, other):
        block = jnp.concatenate([arrived(one), arrived(other)], axis=0)
        gate = dot(block, gate_ref[...])
        upward = dot(block, up_ref[...])
        hidden = (gate / (1.0 + jnp.exp(-gate)) * upward).astype(BF16)
        for b, (i, j) in enumerate(BLOCKS):
            first = hidden[:, i * LANES : (i + 1) * LANES]
            second = hidden[:, j * LANES : (j + 1) * LANES]
            gram[:, b * LANES : (b + 1) * LANES] += dot(first, second, ((0,), (0,)))

    lead(1)
    choose(0, tokens_ref[...], routing_ref[...])
    gram[...] = jnp.zeros_like(gram)
    follow(1)

    def step(d, _):
        lead(d)
        choose(d - 1, held[d - 1], ids[d - 1])
        follow(d)
        choose(zs - d + 1, held[zs - d + 1], ids[zs - d + 1])

        @pl.when(d > 2)
        def _():
            accumulate(d - 2, zs - d + 2)

        return 0

    lax.fori_loop(2, ups - 1, step, 0)
    low, high = ups - 1, ups + 1
    take_ids(low, ups, right)
    take(low, 0, ups, right)
    take_ids(high, None, left)
    take(high, 0, None, left)
    choose(low - 1, held[low - 1], ids[low - 1])
    take(low, 1, None, right)
    take(high, 1, ups, left)
    choose(high + 1, held[high + 1], ids[high + 1])
    choose(low, held[low], ids[low])
    choose(high, held[high], ids[high])
    accumulate(low - 2, high + 2)
    take_ids(ups, None, right)
    take(ups, 0, None, right)
    take(ups, 1, None, left)
    choose(ups, held[ups], ids[ups])
    accumulate(low - 1, high + 1)
    accumulate(low, high)
    accumulate(0, ups)

    def sent(slot, _):
        for part in range(halves):
            token_copy(tokens_ref, slot, part, right).wait_send()
        ids_copy(routing_ref, slot, right).wait_send()
        return 0

    lax.fori_loop(1, zs, sent, 0)


def partner(i, sizes, here, sign):
    ys, zs, cores = sizes
    y, z, c = here
    dc = lax.rem(i, cores)
    rest = i // cores
    dy = lax.rem(rest, ys)
    zi = rest // ys
    dz = lax.rem(lax.rem(zi, 2) * ((zi + 1) // 2) + (1 - lax.rem(zi, 2)) * (zs - zi // 2), zs)
    if sign > 0:
        to = (lax.rem(y + dy, ys), lax.rem(z + dz, zs), lax.rem(c + dc, cores))
    else:
        to = (lax.rem(y + ys - dy, ys), lax.rem(z + zs - dz, zs), lax.rem(c + cores - dc, cores))
    return to, dict(zip(SEQ, to)), (to[0] * zs + to[1]) * cores + to[2]


def inverse(block, pivots=8):
    size = block.shape[0]
    lanes = lax.broadcasted_iota(jnp.int32, (8, size), 1)
    all_lanes = lax.broadcasted_iota(jnp.int32, (size, size), 1)
    subs = lax.broadcasted_iota(jnp.int32, (8, size), 0)

    def spread(x):
        return jnp.broadcast_to(x, (8, size))

    for k in range(0, size, pivots):
        own, row = 8 * (k // 8), k % 8
        rows = block[own : own + 8]
        mine = [spread(rows[:, k + j : k + j + 1]) for j in range(pivots)]
        inside = (lanes >= k) & (lanes < k + pivots)
        y = [
            jnp.where(
                lanes == k + j, 1.0, jnp.where(inside, 0.0, spread(rows[row + j : row + j + 1]))
            )
            for j in range(pivots)
        ]
        a = [[None] * pivots for _ in range(pivots)]
        for i in range(pivots):
            for j in range(i, pivots):
                a[i][j] = spread(mine[j][row + i : row + i + 1])
        d = [None] * pivots
        low = [[None] * pivots for _ in range(pivots)]
        for i in range(pivots):
            d[i] = 1.0 / a[i][i]
            for j in range(i + 1, pivots):
                low[j][i] = a[i][j] * d[i]
            for j in range(i + 1, pivots):
                for m in range(j, pivots):
                    a[j][m] = a[j][m] - low[j][i] * a[i][m]
                y[j] = y[j] - low[j][i] * y[i]
        y = [y[i] * d[i] for i in range(pivots)]
        for i in range(pivots - 1, -1, -1):
            for j in range(i):
                y[j] = y[j] - low[i][j] * y[i]
        fresh = jnp.where((all_lanes >= k) & (all_lanes < k + pivots), 0.0, block)
        for j in range(pivots):
            fresh = fresh - block[:, k + j : k + j + 1] * y[j][:1]
        fixed = fresh[own : own + 8]
        for j in range(pivots):
            fixed = jnp.where(subs == row + j, y[j], fixed)
        pieces = [fresh[:own], fixed, fresh[own + 8 :]]
        block = jnp.concatenate([p for p in pieces if p.shape[0]], axis=0)
    return block


def square(which):
    return lax.broadcasted_iota(jnp.int32, (LANES, LANES), which)


def fold(blocks):
    a00, a10, a11, a20, a21, a22 = blocks
    row, col = square(0), square(1)
    diagonal = jnp.sum(jnp.where(row == col, a11, 0.0), axis=0, keepdims=True)
    spare = jnp.where(row == 0, diagonal, 0.0)
    spare = jnp.where((row == 1) & (col == 2), diagonal[:, :1], spare)
    return (a10, a20, jnp.where(row >= col, a00, a11)), (a21, jnp.where(row >= col, a22, spare))


def lower_of(x):
    row, col = square(0), square(1)
    return jnp.where(row >= col, x, 0.0) + jnp.where(row > col, x, 0.0).T


def solve(first, rest, right):
    nt, tn = ((1,), (1,)), ((0,), (0,))
    row, col = square(0), square(1)
    a10, a20, mixed = first()
    d0 = inverse(lower_of(mixed))
    l10 = dot(a10, d0, precision=HI)
    l20 = dot(a20, d0, precision=HI)
    y1 = right[1] - dot(l10, right[0], precision=HI)
    z0 = dot(d0, right[0], precision=HI)
    down11 = dot(l10, a10, nt, precision=HI)
    down21 = dot(l20, a10, nt, precision=HI)
    down22 = dot(l20, a20, nt, precision=HI)
    above = jnp.where(row < col, mixed, 0.0)
    above = above + above.T
    a21, last = rest()
    diagonal = jnp.where(col[:1] == 0, last[1:2, 2:3], last[:1])
    a11 = above + jnp.where(row == col, diagonal, 0.0) - down11
    d1 = inverse(a11)
    a21 = a21 - down21
    a22 = lower_of(last) - down22
    l21 = dot(a21, d1, precision=HI)
    a22 = a22 - dot(l21, a21, nt, precision=HI)
    d2 = inverse(a22)
    y2 = right[2] - dot(l20, right[0], precision=HI) - dot(l21, y1, precision=HI)
    z1 = dot(d1, y1, precision=HI)
    x2 = dot(d2, y2, precision=HI)
    yield 2, x2
    x1 = z1 - dot(l21, x2, tn, precision=HI)
    yield 1, x1
    yield 0, z0 - dot(l10, x1, tn, precision=HI) - dot(l20, x2, tn, precision=HI)


def as_column(row, count, repeat=1):
    size = row.shape[1]
    shape = (count * repeat, size)
    hit = lax.broadcasted_iota(jnp.int32, shape, 0) // repeat == lax.broadcasted_iota(
        jnp.int32, shape, 1
    )
    return jnp.sum(jnp.where(hit, jnp.broadcast_to(row, shape), 0.0), axis=1, keepdims=True)


def tables(cluster_ref, owners_ref, ways):
    cluster = cluster_ref[...].astype(F32)
    owners = owners_ref[...].astype(F32)
    experts, clusters = cluster.shape[1], owners.shape[1]
    same = (as_column(cluster, experts) == cluster).astype(F32)

    owner = as_column(owners, clusters)
    square = (clusters, clusters)
    earlier = lax.broadcasted_iota(jnp.int32, square, 1) < lax.broadcasted_iota(jnp.int32, square, 0)
    ranking = jnp.sum(jnp.where((owner == owners) & earlier, 1.0, 0.0), axis=1, keepdims=True)
    slots = owner * OWN + ranking
    shape = (clusters, experts)
    member = lax.broadcasted_iota(jnp.int32, shape, 0).astype(F32) == cluster
    member_slot = jnp.sum(jnp.where(member, slots, 0.0), axis=0, keepdims=True)

    shape = (experts * ways, experts)
    row = lax.broadcasted_iota(jnp.int32, shape, 0)
    mine = as_column(cluster, experts, ways) == cluster
    held = member_slot == (row // ways).astype(F32)
    router = jnp.where(row % ways == 0, mine.astype(F32), held.astype(F32)).astype(BF16)
    return same, router


def merge_kernel(sizes, tokens_ref, routing_ref, gate_ref, up_ref, down_ref, cluster_ref,
                 owners_ref, b_in, gram, whole, g_out, g_in, s_out, s_in,
                 m_out, m_in, wide, mixed, b_out,
                 g_sems, s_sems, m_sems, b_sems, local_sem, *spread):
    n = sizes[0] * sizes[1] * sizes[2]
    here = tuple(lax.axis_index(x) for x in SEQ)
    me = (here[0] * sizes[1] + here[1]) * sizes[2] + here[2]
    blocks = len(BLOCKS)
    per = (3, 2)
    cuts = len(per)
    size, width = down_ref.shape
    wide_groups = width // LANES
    parts = size // LANES
    tall = LANES // 8

    gather_gram(sizes, tokens_ref, routing_ref, gate_ref, up_ref, gram, *spread)
    eye = (
        lax.broadcasted_iota(jnp.int32, (LANES, LANES), 0)
        == lax.broadcasted_iota(jnp.int32, (LANES, LANES), 1)
    ).astype(F32)
    for b, (i, j) in enumerate(BLOCKS):
        if i == j:
            gram[:, b * LANES : (b + 1) * LANES] += ridge_weight * eye
    own = [gram[:, b * LANES : (b + 1) * LANES] for b in range(blocks)]
    for h, squares in enumerate(fold(own)):
        for k in range(per[h]):
            g_out[h, pl.ds(k, n, stride=8), :] = squares[k]

    def send(src, dst, sems, h):
        own = pltpu.make_async_copy(src(me), dst(me), local_sem)
        own.start()

        def one(i, _):
            _, to, index = partner(n - i, sizes, here, 1)
            pltpu.make_async_remote_copy(
                src_ref=src(index), dst_ref=dst(me), send_sem=sems.at[0, h], recv_sem=sems.at[1, h],
                device_id=to, device_id_type=MESH).start()
            return 0

        lax.fori_loop(1, n, one, 0)
        own.wait()

    def settle(ref, sems, h):
        pltpu.make_async_remote_copy(
            src_ref=ref, dst_ref=ref, send_sem=sems.at[0, h], recv_sem=sems.at[1, h],
            device_id={"seq_0": 0}, device_id_type=MESH).wait()

    def lines(ref, h):
        return lambda i: ref.at[h, pl.ds(pl.multiple_of(i * 8, 8), per[h]), :]

    def settle_lines(ref, sems, h):
        settle(ref.at[h, pl.ds(0, (n - 1) * per[h]), :], sems, h)

    for h in range(cuts):
        send(lines(g_out, h), lines(g_in, h), g_sems, h)

    ways = b_in.shape[2]
    same, router = tables(cluster_ref, owners_ref, ways)
    whole[0] = jnp.concatenate([own[0], own[1].T, own[3].T], axis=1)
    whole[1] = jnp.concatenate([own[1], own[2], own[4].T], axis=1)
    whole[2] = jnp.concatenate([own[3], own[4], own[5]], axis=1)
    for h in range(cuts):
        settle_lines(g_in, g_sems, h)
        for k in range(per[h]):
            s_out[h, pl.ds(k, n, stride=8), :] = dot(
                same, g_in[h, pl.ds(k, n, stride=8), :], precision=HI)
        send(lines(s_out, h), lines(s_in, h), s_sems, h)

    def summed(h):
        settle_lines(s_in, s_sems, h)
        return [s_in[h, pl.ds(k, n, stride=8), :] for k in range(per[h])]

    solved = solve(lambda: summed(0), lambda: summed(1), [whole[i] for i in range(parts)])
    down = down_ref[...]
    order = []
    for p, x in solved:
        order.append(p)
        high = x.astype(BF16)
        low = (x - high.astype(F32)).astype(BF16)
        part = dot(high, down) + dot(low, down)
        for g in range(tall):
            for c in range(wide_groups):
                m_out[p, g * wide_groups + c] = part[
                    g * 8 : g * 8 + 8, c * LANES : (c + 1) * LANES].astype(BF16)
        send(lambda i: m_out.at[p, i], lambda i: m_in.at[p, i], m_sems, p)

    for p in order:
        settle(m_in.at[p, pl.ds(0, n - 1)], m_sems, p)

        def widen(i, _):
            wide[pl.ds(pl.multiple_of(i * 8, 8), 8), :] = m_in[p, i].astype(F32)
            return 0

        lax.fori_loop(0, n, widen, 0, unroll=8)

        def mix(r, _):
            x = wide[pl.ds(r, n, stride=8), :].astype(BF16)
            mixed[pl.ds(r, ways * n, stride=8), :] = dot(router, x)
            return 0

        lax.fori_loop(0, 8, mix, 0, unroll=4)

        def narrow(i, _):
            for w in range(ways):
                b_out[p, i, w] = mixed[pl.ds(pl.multiple_of((i * ways + w) * 8, 8), 8), :].astype(BF16)
            return 0

        lax.fori_loop(0, n, narrow, 0, unroll=4)
        send(lambda i: b_out.at[p, i], lambda i: b_in.at[p, i], b_sems, p)

    for p in order:
        settle(b_in.at[p, pl.ds(0, n - 1)], b_sems, p)


def merge(tokens, routing_t, gate, up, down, cluster_of, owners, sizes, capacity, cuts=2, ways=2):
    ys, zs, cores = sizes
    n = ys * zs * cores
    count = ys * cores
    rows, features = tokens.shape
    size, width = down.shape
    parts = size // LANES
    blocks = len(BLOCKS)
    vm = pl.BlockSpec(memory_space=pltpu.VMEM)
    lines = pltpu.VMEM((cuts, n * 8, LANES), F32)
    dma = pltpu.SemaphoreType.DMA
    return pl.pallas_call(
        functools.partial(merge_kernel, sizes),
        out_shape=jax.ShapeDtypeStruct((parts, n, ways, 8, LANES), BF16),
        in_specs=[vm] * 7,
        out_specs=vm,
        scratch_shapes=[
            pltpu.VMEM((LANES, blocks * LANES), F32),
            pltpu.VMEM((parts, LANES, size), F32),
            lines, lines, lines, lines,
            pltpu.VMEM((parts, n, 8, LANES), BF16),
            pltpu.VMEM((parts, n, 8, LANES), BF16),
            pltpu.VMEM((n * 8, LANES), F32),
            pltpu.VMEM((ways * n * 8, LANES), F32),
            pltpu.VMEM((parts, n, ways, 8, LANES), BF16),
            dma((2, cuts)), dma((2, cuts)), dma((2, parts)), dma((2, parts)), dma,
            pltpu.VMEM((count, zs, capacity, features), BF16),
            pltpu.VMEM((zs, rows, features), BF16),
            pltpu.VMEM((zs,) + routing_t.shape, jnp.int32),
            pltpu.VMEM((zs, count - 1, capacity, features), BF16),
            dma((zs, 2)), dma((zs, 2)), dma((zs,)), dma((zs,)), dma((zs,)), dma((zs,)),
        ],
        compiler_params=pltpu.CompilerParams(collective_id=0, has_side_effects=True),
    )(tokens, routing_t, gate, up, down, cluster_of.reshape(1, -1), owners.reshape(1, -1))


def finish_kernel(chunks_ref, down_ref, diff_ref, slot_ref):
    wide_groups = down_ref.shape[1] // LANES
    for g in range(down_ref.shape[0] // 16):
        rows = slice(g * 16, g * 16 + 16)
        for c in range(wide_groups):
            columns = slice(c * LANES, (c + 1) * LANES)
            upper = g * 2 * wide_groups + c
            mine, held = (
                jnp.concatenate(
                    [chunks_ref[0, upper, w], chunks_ref[0, upper + wide_groups, w]], axis=0)
                for w in range(2)
            )
            diff_ref[rows, columns] = (
                mine.astype(F32) - down_ref[rows, columns].astype(F32)
            ).astype(BF16)
            slot_ref[rows, columns] = held


def finish(chunks, down):
    size, width = down.shape
    block = pl.BlockSpec((LANES, width), lambda p: (p, 0))
    return pl.pallas_call(
        finish_kernel,
        out_shape=(jax.ShapeDtypeStruct((size, width), BF16),) * 2,
        grid=(chunks.shape[0],),
        in_specs=[pl.BlockSpec((1,) + chunks.shape[1:], lambda p: (p, 0, 0, 0, 0)), block],
        out_specs=(block, block),
    )(chunks, down)


def body(tokens, routing, gate_weight, up_weight, down_weight, cluster_of, owners):
    ys, zs, cores = (lax.axis_size(a) for a in SEQ)
    rows_dev = tokens.shape[0]
    topk = routing.shape[1]
    experts = cluster_of.shape[0]
    capacity = min(rows_dev, max(2, 2 * rows_dev * topk // experts))

    chunks = merge(
        tokens, routing.T, gate_weight[0], up_weight[0], down_weight[0], cluster_of, owners,
        (ys, zs, cores), capacity)
    differences, merged_slots = finish(chunks, down_weight[0])
    return (differences[None], merged_slots[None])


def solution(mesh):
    finer = Mesh(
        mesh.devices.reshape(4, 16, 2, mesh.shape["layer"]), ("seq_0", "seq_1", "seq_2", "layer")
    )
    return jax.shard_map(
        body,
        mesh=finer,
        in_specs=(
            P(LAYER_SEQ, None),
            P(LAYER_SEQ, None),
            P(LAYER_SEQ, None, None),
            P(LAYER_SEQ, None, None),
            P(LAYER_SEQ, None, None),
            P("layer"),
            P("layer"),
        ),
        out_specs=(P(LAYER_SEQ, None, None), P(LAYER_SEQ, None, None)),
        check_vma=False,
    )
```
